512 devices in a mesh: wide: 32 (over z, y_hi), narrow: 16 (over x, y_lo, core).
Axes of the slice: x: 4, y: 4 (y_hi: 2, y_lo: 2; y = y_hi * 2 + y_lo), z: 16, core: 2. Of those that a mesh axis runs over, the one named last changes fastest.
Arguments:
- embed: bfloat16 [393216, 1024], P(('wide', 'narrow')), may hold values from -6 to 6
- dest: int32 [393216], P(('wide', 'narrow')), may hold values from 0 to 15, as said below
- means: bfloat16 [4096, 1024], P('narrow'), may hold values from -3 to 3
- variances: bfloat16 [4096, 1024], P('narrow'), may hold values from 0.5 to 2
Outputs:
- new_means: float32 [4096, 1024], P('narrow')
- new_variances: float32 [4096, 1024], P('narrow')
The draws below stay inside these ranges and needn't reach their ends.
Inputs may be any that keep to these rules, and one draw needn't show every extreme that they name: `dest`: among the rows of one device, each group number appears exactly 768 / 16 times.
All inputs are finite; a program needn't handle non-finite values.
Results may differ from the reference program's by a relative error of at most 0.00045.
The reference program's roundings to bfloat16 on the way count: a program that leaves them out, or rounds other values in their place, can miss the bound.
Values may be sent and summed in bfloat16 or wider, within the bound.
No kernel may reach another device: no remote copies, remote signals or barrier semaphores. Data moves between devices by JAX's collectives and lax.ppermute only.
A program may use at most 64 MiB of HBM per device.

```python
import math
import jax
import jax.numpy as jnp
from jax import lax

D = 1024
K = 4096
SINK = 3
ROW_DEV = 768
ROWS = 393216
N_NARROW = 16
DEVICES = 512


def draw_dest(key, part):
    keys = jax.random.split(jax.random.fold_in(key, 11), DEVICES)
    orders = jax.vmap(lambda single: jax.random.permutation(single, ROW_DEV))(keys)
    return (orders % N_NARROW).astype(jnp.int32).reshape(DEVICES * ROW_DEV)


def draw_embed(key, part):
    base_key = jax.random.fold_in(key, 23)
    normal_key = jax.random.fold_in(base_key, 0)
    values = jax.random.truncated_normal(normal_key, -6.0, 6.0, (ROWS, D), jnp.float32)
    return values.astype(jnp.bfloat16)


def shard_levels(own_key, dims, cuts, least, largest):
    def one(dim, parts):
        heights = jax.random.uniform(jax.random.fold_in(jax.random.fold_in(own_key, 6), dim), (parts,), jnp.float32, least / len(cuts), largest / len(cuts))
        return jnp.repeat(jnp.exp(heights), dims[dim] // parts).reshape((-1,) + (1,) * (len(dims) - dim - 1))

    loudness = one(*cuts[0])
    for cut in cuts[1:]:
        loudness = loudness * one(*cut)
    return loudness


def centred(rng, extent, deviation, reach, cuts=(), kind=jnp.bfloat16):
    array = deviation * jax.random.normal(rng, extent, jnp.float32)
    if cuts:
        array = array * shard_levels(rng, extent, cuts, -0.22, 0.18)
    return jnp.clip(array, -reach, reach).astype(kind)


def setup_inputs(seed: int = 0) -> dict:
    key_of = jax.random.split(jax.random.key(seed), 5)
    embed = draw_embed(jax.random.fold_in(key_of[4], 71), 0)
    dest = draw_dest(jax.random.fold_in(key_of[4], 71), 0)
    means = centred(key_of[2], (K, D), 0.5, 3.0, ((0, 16),))
    variances = jnp.clip(jnp.exp(math.log(2.0) - 1.3862944 * jax.random.uniform(key_of[3], (K, D), jnp.float32) ** shard_levels(key_of[3], (K, D), ((0, 16),), -0.2, 0.2)), 0.5, 2.0).astype(jnp.bfloat16)
    return {"embed": embed, "dest": dest, "means": means, "variances": variances}


def score_rows(rows, mean_block, var_block):
    prec = 1.0 / var_block.astype(jnp.float32)
    mean_wide = mean_block.astype(jnp.float32)
    quad = (-0.5 * prec).astype(jnp.bfloat16)
    linear = (mean_wide * prec).astype(jnp.bfloat16)
    offset = -0.5 * jnp.sum(jnp.log(var_block.astype(jnp.float32)) + mean_wide * mean_wide * prec, axis=1)
    squared = (rows.astype(jnp.float32) * rows.astype(jnp.float32)).astype(jnp.bfloat16)
    stacked = jnp.concatenate([squared, rows], axis=1)
    weights = jnp.concatenate([quad, linear], axis=1)
    raw = lax.dot_general(stacked, weights, (((1,), (1,)), ((), ())), preferred_element_type=jnp.float32)
    scale = rows.shape[1] ** -0.5
    return scale * (raw + offset[None, :])


def moments(resp, rows):
    values = rows.astype(jnp.float32)
    first = lax.dot_general(resp, values, (((0,), (0,)), ((), ())), precision=lax.Precision.HIGHEST, preferred_element_type=jnp.float32)
    second = lax.dot_general(resp, values * values, (((0,), (0,)), ((), ())), precision=lax.Precision.HIGHEST, preferred_element_type=jnp.float32)
    return first, second


def reference(embed, dest, means, variances):
    groups = N_NARROW
    block = ROW_DEV // groups
    comp = K // groups
    by_device = embed.reshape(DEVICES, ROW_DEV, D)
    order = jnp.argsort(dest.reshape(DEVICES, ROW_DEV), axis=1, stable=True).astype(jnp.int32)
    group_rows = DEVICES * block

    def one_group(group):
        start = (group * block).astype(jnp.int32)
        picks = lax.dynamic_slice_in_dim(order, start, block, 1)
        rows = jnp.take_along_axis(by_device, picks[:, :, None], axis=1).reshape(group_rows, D)
        first_comp = (group * comp).astype(jnp.int32)
        mean_block = lax.dynamic_slice_in_dim(means, first_comp, comp, 0)
        var_block = lax.dynamic_slice_in_dim(variances, first_comp, comp, 0)
        score = score_rows(rows, mean_block, var_block)
        resp = jax.nn.softmax(score, axis=1)
        target = jnp.float32(group_rows / comp)
        for step in range(SINK):
            mass = jnp.sum(resp, axis=0)
            resp = resp * (target / mass)[None, :]
            resp = resp / jnp.sum(resp, axis=1, keepdims=True)
        total = jnp.sum(resp, axis=0)
        first, second = moments(resp, rows)
        new_mean = first / total[:, None]
        new_var = second / total[:, None] - new_mean * new_mean + 0.01
        return new_mean, new_var

    new_means, new_variances = lax.map(one_group, jnp.arange(groups, dtype=jnp.int32))
    return new_means.reshape(K, D), new_variances.reshape(K, D)
```

```python
import jax
import jax.numpy as jnp
from jax import lax
from jax.sharding import PartitionSpec as P

SINK = 3
PAD = 128


def score_rows(rows, mean_block, var_block):
    prec = 1.0 / var_block.astype(jnp.float32)
    mean_wide = mean_block.astype(jnp.float32)
    quad = (-0.5 * prec).astype(jnp.bfloat16)
    linear = (mean_wide * prec).astype(jnp.bfloat16)
    offset = -0.5 * jnp.sum(
        jnp.log(var_block.astype(jnp.float32)) + mean_wide * mean_wide * prec, axis=1
    )
    squared = (rows.astype(jnp.float32) * rows.astype(jnp.float32)).astype(jnp.bfloat16)
    stacked = jnp.concatenate([squared, rows], axis=1)
    weights = jnp.concatenate([quad, linear], axis=1)
    raw = lax.dot_general(
        stacked, weights, (((1,), (1,)), ((), ())), preferred_element_type=jnp.float32
    )
    scale = rows.shape[1] ** (-0.5)
    return scale * (raw + offset[None, :])


def sum_small(part, members):
    block = part.reshape(1, -1, 128)
    sent = jnp.broadcast_to(block, (members,) + block.shape[1:])
    got = lax.all_to_all(sent, "wide", split_axis=0, concat_axis=0, tiled=True)
    return jnp.sum(got, axis=0).reshape(part.shape)


def with_total(values, total):
    high = lax.reduce_precision(total, 5, 10)
    low = total - high
    lane = lax.broadcasted_iota(jnp.int32, (values.shape[0], PAD), 1)
    tail = jnp.where(lane < PAD // 2, high[:, None], low[:, None])
    return jnp.concatenate([values, tail], axis=1).astype(jnp.float16)


def split_total(payload):
    moments = payload.shape[1] - PAD
    return payload[:, :moments], payload[:, moments] + payload[:, moments + PAD // 2]


def on_device(embed, dest, means, variances):
    rows_dev, width = embed.shape
    groups = lax.axis_size("narrow")
    members = lax.axis_size("wide")
    block = rows_dev // groups
    comp = means.shape[0]
    deep = members // 2
    pairs = [[2 * z, 2 * z + 1] for z in range(deep)]
    lines = [[2 * z + y for z in range(deep)] for y in range(2)]
    order = jnp.argsort(dest, stable=True)
    ordered = embed[order].reshape(groups, block, width)
    arrived = lax.all_to_all(ordered, "narrow", split_axis=0, concat_axis=0, tiled=True).reshape(
        rows_dev, width
    )
    score = score_rows(arrived, means, variances)
    resp = jax.nn.softmax(score, axis=1)
    target = jnp.float32(rows_dev * members / comp)
    for step in range(SINK):
        mass = sum_small(jnp.sum(resp, axis=0), members)
        scaled = resp * (target / mass)[None, :]
        resp = scaled / jnp.sum(scaled, axis=1, keepdims=True)
    values = arrived.astype(jnp.float32)
    both = jnp.concatenate([values, values * values], axis=1)
    sums = lax.dot_general(
        resp,
        both,
        (((0,), (0,)), ((), ())),
        precision=lax.Precision.HIGHEST,
        preferred_element_type=jnp.float32,
    )
    sent = with_total(sums, jnp.sum(resp, axis=0)).reshape(2, comp // 2, 2 * width + PAD)
    got = lax.all_to_all(
        sent, "wide", split_axis=0, concat_axis=0, tiled=True, axis_index_groups=pairs
    )
    sums, total = split_total(jnp.sum(got.astype(jnp.float32), axis=0))
    sent = with_total(sums, total).reshape(deep, comp // members, 2 * width + PAD)
    got = lax.all_to_all(
        sent, "wide", split_axis=0, concat_axis=0, tiled=True, axis_index_groups=lines
    )
    sums, total = split_total(jnp.sum(got.astype(jnp.float32), axis=0))
    new_mean = sums[:, :width] / total[:, None]
    new_var = sums[:, width:] / total[:, None] - new_mean * new_mean + 0.01
    mine = jnp.concatenate([new_mean, new_var], axis=1).astype(jnp.float16)
    sent = jnp.broadcast_to(mine[None], (deep,) + mine.shape)
    got = lax.all_to_all(
        sent, "wide", split_axis=0, concat_axis=0, tiled=True, axis_index_groups=lines
    )
    half = got.reshape(1, comp // 2, 2 * width)
    sent = jnp.broadcast_to(half, (2,) + half.shape[1:])
    got = lax.all_to_all(
        sent, "wide", split_axis=0, concat_axis=0, tiled=True, axis_index_groups=pairs
    )
    out = got.reshape(comp, 2 * width).astype(jnp.float32)
    return (out[:, :width], out[:, width:])


def solution(mesh):
    return jax.shard_map(
        on_device,
        mesh=mesh,
        in_specs=(
            P(("wide", "narrow"), None),
            P(("wide", "narrow")),
            P("narrow", None),
            P("narrow", None),
        ),
        out_specs=(P("narrow", None), P("narrow", None)),
        check_vma=False,
    )
```

```python
import functools

import jax
import jax.numpy as jnp
from jax import lax
from jax.experimental import pallas as pl
from jax.experimental.pallas import tpu as pltpu
from jax.sharding import PartitionSpec as P

SINK = 3
LANES = 128
ROW_STEP = 256
F32 = jnp.float32
BF16 = jnp.bfloat16
VMEM_LIMIT = 40 * 1024 * 1024


def call(kernel, out_shape, n_in, flops, moved, scalars=0, scratch=()):
    smem = pl.BlockSpec(memory_space=pltpu.SMEM)
    vmem = pl.BlockSpec(memory_space=pltpu.VMEM)
    return pl.pallas_call(
        kernel,
        out_shape=out_shape,
        in_specs=[smem] * scalars + [vmem] * n_in,
        out_specs=jax.tree.map(lambda _: vmem, out_shape),
        scratch_shapes=scratch,
        compiler_params=pltpu.CompilerParams(vmem_limit_bytes=VMEM_LIMIT),
        cost_estimate=pl.CostEstimate(flops=flops, bytes_accessed=moved, transcendentals=0),
    )


def dot_nt(a, b):
    return lax.dot_general(a, b, (((1,), (1,)), ((), ())), preferred_element_type=F32)


def dot_tn(a, b):
    return lax.dot_general(a, b, (((0,), (0,)), ((), ())), preferred_element_type=F32)


def order_kernel(groups, dest_ref, embed_ref, out_ref):
    rows = embed_ref.shape[0]
    block = rows // groups
    before = lax.broadcasted_iota(jnp.int32, (LANES, LANES), 0)
    after = lax.broadcasted_iota(jnp.int32, (LANES, LANES), 1)
    earlier = jnp.where(before < after, 1.0, 0.0).astype(BF16)
    group = lax.broadcasted_iota(jnp.int32, (groups, LANES), 0)
    base = (group * block).astype(F32)
    count = jnp.zeros((groups, 1), F32)
    places = []
    for start in range(0, rows, LANES):
        hot = jnp.where(group == dest_ref[:, start : start + LANES], 1.0, 0.0)
        rank = jnp.dot(hot.astype(BF16), earlier, preferred_element_type=F32) + count
        places.append(jnp.sum(hot * (rank + base), axis=0, keepdims=True))
        count = count + jnp.sum(hot, axis=1, keepdims=True)
    place = jnp.concatenate(places, axis=1).astype(jnp.int32)
    for start in range(0, rows, ROW_STEP):
        slot = lax.broadcasted_iota(jnp.int32, (ROW_STEP, rows), 0) + start
        pick = jnp.where(slot == place, 1.0, 0.0).astype(BF16)
        got = jnp.dot(pick, embed_ref[...], preferred_element_type=F32)
        out_ref[start : start + ROW_STEP, :] = got.astype(BF16)


def put_mass(mass, sent_ref):
    comp = mass.shape[1]
    parts = [mass[:, s : s + LANES] for s in range(0, comp, LANES)]
    block = jnp.concatenate(parts + [jnp.zeros((8 - len(parts), LANES), F32)], axis=0)
    sent_ref[...] = jnp.broadcast_to(block[None], sent_ref.shape)


def get_mass(got_ref, comp):
    block = jnp.sum(got_ref[...], axis=0)
    return jnp.concatenate([block[i : i + 1] for i in range(comp // LANES)], axis=1)


def score_step(x, quad_ref, lin_ref, off_ref, scale):
    wide = x.astype(F32)
    raw = dot_nt((wide * wide).astype(BF16), quad_ref[...]) + dot_nt(x, lin_ref[...])
    score = scale * (raw + off_ref[...])
    lifted = jnp.exp(score - jnp.max(score, axis=1, keepdims=True))
    return lifted / jnp.sum(lifted, axis=1, keepdims=True)


def score_kernel(scale, x_ref, quad_ref, lin_ref, off_ref, resp_ref, sent_ref=None):
    rows = x_ref.shape[0]
    mass = jnp.zeros((1, resp_ref.shape[1]), F32)
    for start in range(0, rows, ROW_STEP):
        span = slice(start, start + ROW_STEP)
        resp = score_step(x_ref[span, :], quad_ref, lin_ref, off_ref, scale)
        resp_ref[span, :] = resp
        mass = mass + jnp.sum(resp, axis=0, keepdims=True)
    if sent_ref is not None:
        put_mass(mass, sent_ref)


def balance_step(resp, pull):
    scaled = resp * pull
    return scaled / jnp.sum(scaled, axis=1, keepdims=True)


def balance_kernel(target, got_ref, resp_ref, out_ref, sent_ref=None):
    rows, comp = resp_ref.shape
    pull = target / get_mass(got_ref, comp)
    mass = jnp.zeros((1, comp), F32)
    for start in range(0, rows, ROW_STEP):
        span = slice(start, start + ROW_STEP)
        resp = balance_step(resp_ref[span, :], pull)
        out_ref[span, :] = resp
        mass = mass + jnp.sum(resp, axis=0, keepdims=True)
    if sent_ref is not None:
        put_mass(mass, sent_ref)


def moment_kernel(
    target, side_ref, got_ref, mine_ref, theirs_ref, x_ref, y_ref, first_ref, second_ref, total_ref
):
    rows, comp = mine_ref.shape
    half = comp // 2
    width = x_ref.shape[1]
    pull = target / get_mass(got_ref, comp)
    upper = side_ref[0] == 1
    first = jnp.zeros((2 * half, width), F32)
    second = jnp.zeros((2 * half, width), F32)
    third = jnp.zeros((half, width), F32)
    total = jnp.zeros((2 * half, LANES), F32)
    ones = jnp.ones((ROW_STEP, LANES), BF16)
    for resp_ref, rows_ref in ((mine_ref, x_ref), (theirs_ref, y_ref)):
        for start in range(0, rows, ROW_STEP):
            span = slice(start, start + ROW_STEP)
            resp = balance_step(resp_ref[span, :], pull)
            resp = jnp.where(upper, resp[:, half:], resp[:, :half])
            high = resp.astype(BF16)
            low = (resp - high.astype(F32)).astype(BF16)
            both = jnp.concatenate([high, low], axis=1)
            x = rows_ref[span, :]
            wide = x.astype(F32)
            square = wide * wide
            square_high = square.astype(BF16)
            square_low = (square - square_high.astype(F32)).astype(BF16)
            first = first + dot_tn(both, x)
            second = second + dot_tn(both, square_high)
            third = third + dot_tn(high, square_low)
            total = total + dot_tn(both, ones)
    first_ref[...] = first[:half] + first[half:]
    second_ref[...] = second[:half] + second[half:] + third
    total_ref[...] = total[:half] + total[half:]


def weights(mean_block, var_block):
    prec = 1.0 / var_block.astype(F32)
    mean_wide = mean_block.astype(F32)
    quad = (-0.5 * prec).astype(BF16)
    linear = (mean_wide * prec).astype(BF16)
    offset = -0.5 * jnp.sum(
        jnp.log(var_block.astype(F32)) + mean_wide * mean_wide * prec, axis=1
    )
    return quad, linear, offset[None, :]


def with_total(first, second, total):
    high = lax.reduce_precision(total, 5, 10)
    lane = lax.broadcasted_iota(jnp.int32, total.shape, 1)
    tail = jnp.where(lane < LANES // 2, high, total - high)
    return jnp.concatenate([first, second, tail], axis=1).astype(jnp.float16)


def on_device(embed, dest, means, variances):
    rows_dev, width = embed.shape
    groups = lax.axis_size("narrow")
    members = lax.axis_size("wide")
    block = rows_dev // groups
    comp = means.shape[0]
    half = comp // 2
    deep = members // 2
    pairs = [[2 * z, 2 * z + 1] for z in range(deep)]
    lines = [[2 * z + y for z in range(deep)] for y in range(2)]
    swap = [(i, i ^ 1) for i in range(members)]
    side = (lax.axis_index("wide") % 2).astype(jnp.int32).reshape(1)
    scale = width ** (-0.5)
    target = float(rows_dev * members / comp)
    big = rows_dev * width
    area = rows_dev * comp

    everyone = functools.partial(
        lax.all_to_all, axis_name="wide", split_axis=0, concat_axis=0, tiled=True
    )
    resp_shape = jax.ShapeDtypeStruct((rows_dev, comp), F32)
    sent_shape = jax.ShapeDtypeStruct((members, 8, LANES), F32)

    ordered = call(
        functools.partial(order_kernel, groups),
        jax.ShapeDtypeStruct(embed.shape, BF16), 2, 2 * rows_dev * big, 4 * big,
    )(dest.reshape(1, rows_dev), embed)
    mine = lax.all_to_all(
        ordered.reshape(groups, block, width), "narrow", split_axis=0, concat_axis=0, tiled=True
    ).reshape(rows_dev, width)
    theirs = lax.ppermute(mine, "wide", swap)
    quad, linear, offset = weights(means, variances)
    resp, sent = call(
        functools.partial(score_kernel, scale), (resp_shape, sent_shape),
        4, 4 * big * comp, 2 * big + 4 * area,
    )(mine, quad, linear, offset)
    got = everyone(sent)
    other = call(
        functools.partial(score_kernel, scale), resp_shape,
        4, 4 * big * comp, 2 * big + 4 * area,
    )(theirs, quad, linear, offset)
    for step in range(SINK - 1):
        last = got
        resp, sent = call(
            functools.partial(balance_kernel, target), (resp_shape, sent_shape),
            2, 4 * area, 8 * area,
        )(last, resp)
        got = everyone(sent)
        other = call(
            functools.partial(balance_kernel, target), resp_shape, 2, 4 * area, 8 * area,
        )(last, other)
    first, second, total = call(
        functools.partial(moment_kernel, target),
        (
            jax.ShapeDtypeStruct((half, width), F32),
            jax.ShapeDtypeStruct((half, width), F32),
            jax.ShapeDtypeStruct((half, LANES), F32),
        ),
        5, 10 * big * comp, 4 * big + 8 * area, scalars=1,
    )(side, got, resp, other, mine, theirs)
    sent = with_total(first, second, total).reshape(deep, comp // members, 2 * width + LANES)
    got = everyone(sent, axis_index_groups=lines)
    sums = jnp.sum(got.astype(F32), axis=0)
    total = (sums[:, 2 * width] + sums[:, 2 * width + LANES // 2])[:, None]
    new_mean = sums[:, :width] / total
    new_var = sums[:, width : 2 * width] / total - new_mean * new_mean + 0.01
    done = jnp.concatenate([new_mean, new_var], axis=1).astype(jnp.float16)
    got = everyone(jnp.broadcast_to(done[None], (deep,) + done.shape), axis_index_groups=lines)
    got = got.reshape(1, half, 2 * width)
    got = everyone(jnp.broadcast_to(got, (2,) + got.shape[1:]), axis_index_groups=pairs)
    out = got.reshape(comp, 2 * width).astype(F32)
    return (out[:, :width], out[:, width:])


def solution(mesh):
    return jax.shard_map(
        on_device,
        mesh=mesh,
        in_specs=(
            P(("wide", "narrow"), None),
            P(("wide", "narrow")),
            P("narrow", None),
            P("narrow", None),
        ),
        out_specs=(P("narrow", None), P("narrow", None)),
        check_vma=False,
    )
```

```python
import functools

import jax
import jax.numpy as jnp
from jax import lax
from jax.experimental import pallas as pl
from jax.experimental.pallas import tpu as pltpu
from jax.sharding import PartitionSpec as P

SINK = 3
LANES = 128
ROW_STEP = 256
F32 = jnp.float32
BF16 = jnp.bfloat16
VMEM_LIMIT = 40 * 1024 * 1024


def call(kernel, out_shape, n_in, flops, moved, scalars=0, scratch=()):
    smem = pl.BlockSpec(memory_space=pltpu.SMEM)
    vmem = pl.BlockSpec(memory_space=pltpu.VMEM)
    return pl.pallas_call(
        kernel,
        out_shape=out_shape,
        in_specs=[smem] * scalars + [vmem] * n_in,
        out_specs=jax.tree.map(lambda _: vmem, out_shape),
        scratch_shapes=scratch,
        compiler_params=pltpu.CompilerParams(vmem_limit_bytes=VMEM_LIMIT),
        cost_estimate=pl.CostEstimate(flops=flops, bytes_accessed=moved, transcendentals=0),
    )


def dot_nt(a, b):
    return lax.dot_general(a, b, (((1,), (1,)), ((), ())), preferred_element_type=F32)


def dot_tn(a, b):
    return lax.dot_general(a, b, (((0,), (0,)), ((), ())), preferred_element_type=F32)


def order_kernel(groups, dest_ref, embed_ref, out_ref):
    rows = embed_ref.shape[0]
    block = rows // groups
    before = lax.broadcasted_iota(jnp.int32, (LANES, LANES), 0)
    after = lax.broadcasted_iota(jnp.int32, (LANES, LANES), 1)
    earlier = jnp.where(before < after, 1.0, 0.0).astype(BF16)
    group = lax.broadcasted_iota(jnp.int32, (groups, LANES), 0)
    base = (group * block).astype(F32)
    count = jnp.zeros((groups, 1), F32)
    places = []
    for start in range(0, rows, LANES):
        hot = jnp.where(group == dest_ref[:, start : start + LANES], 1.0, 0.0)
        rank = jnp.dot(hot.astype(BF16), earlier, preferred_element_type=F32) + count
        places.append(jnp.sum(hot * (rank + base), axis=0, keepdims=True))
        count = count + jnp.sum(hot, axis=1, keepdims=True)
    place = jnp.concatenate(places, axis=1).astype(jnp.int32)
    for start in range(0, rows, ROW_STEP):
        slot = lax.broadcasted_iota(jnp.int32, (ROW_STEP, rows), 0) + start
        pick = jnp.where(slot == place, 1.0, 0.0).astype(BF16)
        got = jnp.dot(pick, embed_ref[...], preferred_element_type=F32)
        out_ref[start : start + ROW_STEP, :] = got.astype(BF16)


def put_mass(mass, sent_ref):
    comp = mass.shape[1]
    parts = [mass[:, s : s + LANES] for s in range(0, comp, LANES)]
    block = jnp.concatenate(parts + [jnp.zeros((8 - len(parts), LANES), F32)], axis=0)
    sent_ref[...] = jnp.broadcast_to(block[None], sent_ref.shape)


def get_mass(got_ref, comp):
    block = jnp.sum(got_ref[...], axis=0)
    return jnp.concatenate([block[i : i + 1] for i in range(comp // LANES)], axis=1)


def score_step(x, quad_ref, lin_ref, off_ref, scale):
    wide = x.astype(F32)
    raw = dot_nt((wide * wide).astype(BF16), quad_ref[...]) + dot_nt(x, lin_ref[...])
    score = scale * (raw + off_ref[...])
    lifted = jnp.exp(score - jnp.max(score, axis=1, keepdims=True))
    return lifted / jnp.sum(lifted, axis=1, keepdims=True)


def score_kernel(scale, x_ref, quad_ref, lin_ref, off_ref, resp_ref, sent_ref=None):
    rows = x_ref.shape[0]
    mass = jnp.zeros((1, resp_ref.shape[1]), F32)
    for start in range(0, rows, ROW_STEP):
        span = slice(start, start + ROW_STEP)
        resp = score_step(x_ref[span, :], quad_ref, lin_ref, off_ref, scale)
        resp_ref[span, :] = resp
        mass = mass + jnp.sum(resp, axis=0, keepdims=True)
    if sent_ref is not None:
        put_mass(mass, sent_ref)


def balance_step(resp, pull):
    scaled = resp * pull
    return scaled / jnp.sum(scaled, axis=1, keepdims=True)


def balance_kernel(target, got_ref, resp_ref, out_ref, sent_ref=None):
    rows, comp = resp_ref.shape
    pull = target / get_mass(got_ref, comp)
    mass = jnp.zeros((1, comp), F32)
    for start in range(0, rows, ROW_STEP):
        span = slice(start, start + ROW_STEP)
        resp = balance_step(resp_ref[span, :], pull)
        out_ref[span, :] = resp
        mass = mass + jnp.sum(resp, axis=0, keepdims=True)
    if sent_ref is not None:
        put_mass(mass, sent_ref)


def square_kernel(x_ref, high_ref, low_ref):
    for start in range(0, x_ref.shape[0], ROW_STEP):
        span = slice(start, start + ROW_STEP)
        wide = x_ref[span, :].astype(F32)
        square = wide * wide
        high = square.astype(BF16)
        high_ref[span, :] = high
        low_ref[span, :] = (square - high.astype(F32)).astype(BF16)


def put_moments(both, x_ref, high_ref, low_ref, first_ref, second_ref, total_ref):
    half = first_ref.shape[0]
    first = dot_tn(both, x_ref[...])
    first_ref[...] = first[:half] + first[half:]
    second = dot_tn(both, high_ref[...])
    second_ref[...] = second[:half] + second[half:] + dot_tn(both[:, :half], low_ref[...])
    total = dot_tn(both, jnp.ones((both.shape[0], LANES), BF16))
    total_ref[...] = total[:half] + total[half:]


def crossed_kernel(
    target, side_ref, got_ref, resp_ref, x_ref, high_ref, low_ref,
    kept_ref, first_ref, second_ref, total_ref, lent_ref,
):
    rows, comp = resp_ref.shape
    half = comp // 2
    upper = side_ref[0] == 1
    pull = target / get_mass(got_ref, comp)
    for start in range(0, rows, ROW_STEP):
        span = slice(start, start + ROW_STEP)
        resp = balance_step(resp_ref[span, :], pull)
        high = resp.astype(BF16).astype(F32)
        low = resp - high
        lower_half = jnp.concatenate([high[:, :half], low[:, :half]], axis=1)
        upper_half = jnp.concatenate([high[:, half:], low[:, half:]], axis=1)
        kept_ref[span, :] = jnp.where(upper, upper_half, lower_half).astype(BF16)
        lent_ref[span, :] = jnp.where(upper, lower_half, upper_half).astype(BF16)
    put_moments(lent_ref[...], x_ref, high_ref, low_ref, first_ref, second_ref, total_ref)


def kept_kernel(kept_ref, x_ref, high_ref, low_ref, first_ref, second_ref, total_ref):
    put_moments(kept_ref[...], x_ref, high_ref, low_ref, first_ref, second_ref, total_ref)


def weights(mean_block, var_block):
    prec = 1.0 / var_block.astype(F32)
    mean_wide = mean_block.astype(F32)
    quad = (-0.5 * prec).astype(BF16)
    linear = (mean_wide * prec).astype(BF16)
    offset = -0.5 * jnp.sum(
        jnp.log(var_block.astype(F32)) + mean_wide * mean_wide * prec, axis=1
    )
    return quad, linear, offset[None, :]


def with_total(first, second, total):
    high = lax.reduce_precision(total, 5, 10)
    lane = lax.broadcasted_iota(jnp.int32, total.shape, 1)
    tail = jnp.where(lane < LANES // 2, high, total - high)
    return jnp.concatenate([first, second, tail], axis=1).astype(jnp.float16)


def split_total(payload, part):
    total = payload[:, 2 * part : 2 * part + 1] + payload[:, 2 * part + LANES // 2 :][:, :1]
    return payload[:, :part], payload[:, part : 2 * part], total


def on_device(embed, dest, means, variances):
    rows_dev, width = embed.shape
    groups = lax.axis_size("narrow")
    members = lax.axis_size("wide")
    block = rows_dev // groups
    comp = means.shape[0]
    half = comp // 2
    deep = members // 2
    lines = [[2 * z + y for z in range(deep)] for y in range(2)]
    swap = [(i, i ^ 1) for i in range(members)]
    upper = lax.axis_index("wide") % 2
    own = upper.astype(jnp.int32).reshape(1)
    scale = width ** (-0.5)
    target = float(rows_dev * members / comp)
    big = rows_dev * width
    area = rows_dev * comp

    everyone = functools.partial(
        lax.all_to_all, axis_name="wide", split_axis=0, concat_axis=0, tiled=True
    )
    resp_shape = jax.ShapeDtypeStruct((rows_dev, comp), F32)
    sent_shape = jax.ShapeDtypeStruct((members, 8, LANES), F32)

    ordered = call(
        functools.partial(order_kernel, groups),
        jax.ShapeDtypeStruct(embed.shape, BF16), 2, 2 * rows_dev * big, 4 * big,
    )(dest.reshape(1, rows_dev), embed)
    mine = lax.all_to_all(
        ordered.reshape(groups, block, width), "narrow", split_axis=0, concat_axis=0, tiled=True
    ).reshape(rows_dev, width)
    quad, linear, offset = weights(means, variances)
    resp, sent = call(
        functools.partial(score_kernel, scale), (resp_shape, sent_shape),
        4, 4 * big * comp, 2 * big + 4 * area,
    )(mine, quad, linear, offset)
    got = everyone(sent)
    for step in range(SINK - 1):
        resp, sent = call(
            functools.partial(balance_kernel, target), (resp_shape, sent_shape),
            2, 4 * area, 8 * area,
        )(got, resp)
        got = everyone(sent)
    plain = jax.ShapeDtypeStruct((rows_dev, width), BF16)
    high, low = call(square_kernel, (plain, plain), 1, 4 * big, 6 * big)(mine)
    sums = (
        jax.ShapeDtypeStruct((half, width), F32),
        jax.ShapeDtypeStruct((half, width), F32),
        jax.ShapeDtypeStruct((half, LANES), F32),
    )
    slab = jax.ShapeDtypeStruct((rows_dev, comp), BF16)
    kept, *lent = call(
        functools.partial(crossed_kernel, target), (slab, *sums), 5, 5 * big * comp,
        6 * big + 8 * area, scalars=1, scratch=[pltpu.VMEM((rows_dev, comp), BF16)],
    )(own, got, resp, mine, high, low)
    there = lax.ppermute(with_total(*lent), "wide", swap)
    here = call(kept_kernel, sums, 4, 5 * big * comp, 6 * big + 2 * area)(kept, mine, high, low)
    first, second, total = split_total(there.astype(F32), width)
    sent = with_total(first + here[0], second + here[1], total + here[2])
    got = everyone(sent.reshape(deep, half // deep, sent.shape[1]), axis_index_groups=lines)
    first, second, total = split_total(jnp.sum(got.astype(F32), axis=0), width)
    new_mean = first / total
    new_var = second / total - new_mean * new_mean + 0.01
    done = jnp.concatenate([new_mean, new_var], axis=1).astype(jnp.float16)
    got = everyone(jnp.broadcast_to(done[None], (deep,) + done.shape), axis_index_groups=lines)
    here = got.reshape(half, 2 * width)
    there = lax.ppermute(here, "wide", swap)
    low = jnp.where(upper == 0, here, there)
    high = jnp.where(upper == 0, there, here)
    out = jnp.concatenate([low, high], axis=0).astype(F32)
    return (out[:, :width], out[:, width:])


def solution(mesh):
    return jax.shard_map(
        on_device,
        mesh=mesh,
        in_specs=(
            P(("wide", "narrow"), None),
            P(("wide", "narrow")),
            P("narrow", None),
            P("narrow", None),
        ),
        out_specs=(P("narrow", None), P("narrow", None)),
        check_vma=False,
    )
```

```python
import functools

import jax
import jax.numpy as jnp
from jax import lax
from jax.experimental import pallas as pl
from jax.experimental.pallas import tpu as pltpu
from jax.sharding import PartitionSpec as P

SINK = 3
LANES = 128
ROW_STEP = 256
SAFE = 0.25
F32 = jnp.float32
BF16 = jnp.bfloat16
VMEM_LIMIT = 24 * 1024 * 1024


def call(kernel, out_shape, n_in, flops, moved, scalars=0, scratch=()):
    smem = pl.BlockSpec(memory_space=pltpu.SMEM)
    vmem = pl.BlockSpec(memory_space=pltpu.VMEM)
    return pl.pallas_call(
        kernel,
        out_shape=out_shape,
        in_specs=[smem] * scalars + [vmem] * n_in,
        out_specs=jax.tree.map(lambda _: vmem, out_shape),
        scratch_shapes=scratch,
        compiler_params=pltpu.CompilerParams(vmem_limit_bytes=VMEM_LIMIT),
        cost_estimate=pl.CostEstimate(flops=flops, bytes_accessed=moved, transcendentals=0),
    )


def dot_nt(a, b):
    return lax.dot_general(a, b, (((1,), (1,)), ((), ())), preferred_element_type=F32)


def dot_tn(a, b):
    return lax.dot_general(a, b, (((0,), (0,)), ((), ())), preferred_element_type=F32)


def order_kernel(groups, dest_ref, embed_ref, out_ref):
    rows = embed_ref.shape[0]
    block = rows // groups
    before = lax.broadcasted_iota(jnp.int32, (LANES, LANES), 0)
    after = lax.broadcasted_iota(jnp.int32, (LANES, LANES), 1)
    earlier = jnp.where(before < after, 1.0, 0.0).astype(BF16)
    group = lax.broadcasted_iota(jnp.int32, (groups, LANES), 0)
    base = (group * block).astype(F32)
    count = jnp.zeros((groups, 1), F32)
    places = []
    for start in range(0, rows, LANES):
        hot = jnp.where(group == dest_ref[:, start : start + LANES], 1.0, 0.0)
        rank = jnp.dot(hot.astype(BF16), earlier, preferred_element_type=F32) + count
        places.append(jnp.sum(hot * (rank + base), axis=0, keepdims=True))
        count = count + jnp.sum(hot, axis=1, keepdims=True)
    place = jnp.concatenate(places, axis=1).astype(jnp.int32)
    for start in range(0, rows, ROW_STEP):
        slot = lax.broadcasted_iota(jnp.int32, (ROW_STEP, rows), 0) + start
        pick = jnp.where(slot == place, 1.0, 0.0).astype(BF16)
        got = jnp.dot(pick, embed_ref[...], preferred_element_type=F32)
        out_ref[start : start + ROW_STEP, :] = got.astype(BF16)


def put_mass(mass, sent_ref):
    for i in range(sent_ref.shape[1]):
        part = mass[:, i * LANES : (i + 1) * LANES]
        sent_ref[:, i, :] = jnp.broadcast_to(part, (sent_ref.shape[0], LANES))


def get_mass(got_ref):
    block = jnp.sum(got_ref[...], axis=0)
    return jnp.concatenate([block[i : i + 1] for i in range(block.shape[0])], axis=1)


def score_step(x, quad_ref, lin_ref, off_ref, scale):
    wide = x.astype(F32)
    raw = dot_nt((wide * wide).astype(BF16), quad_ref[...]) + dot_nt(x, lin_ref[...])
    score = scale * (raw + off_ref[...])
    lifted = jnp.exp(score - jnp.max(score, axis=1, keepdims=True))
    return lifted / jnp.sum(lifted, axis=1, keepdims=True)


def score_kernel(scale, x_ref, quad_ref, lin_ref, off_ref, resp_ref, sent_ref=None):
    rows = x_ref.shape[0]
    mass = jnp.zeros((1, resp_ref.shape[1]), F32)
    for start in range(0, rows, ROW_STEP):
        span = slice(start, start + ROW_STEP)
        resp = score_step(x_ref[span, :], quad_ref, lin_ref, off_ref, scale)
        resp_ref[span, :] = resp
        mass = mass + jnp.sum(resp, axis=0, keepdims=True)
    if sent_ref is not None:
        put_mass(mass, sent_ref)


def balance_step(resp, pull):
    scaled = resp * pull
    return scaled / jnp.sum(scaled, axis=1, keepdims=True)


def balance_kernel(target, got_ref, resp_ref, out_ref, sent_ref=None):
    rows, comp = resp_ref.shape
    pull = target / get_mass(got_ref)
    mass = jnp.zeros((1, comp), F32)
    for start in range(0, rows, ROW_STEP):
        span = slice(start, start + ROW_STEP)
        resp = balance_step(resp_ref[span, :], pull)
        out_ref[span, :] = resp
        mass = mass + jnp.sum(resp, axis=0, keepdims=True)
    if sent_ref is not None:
        put_mass(mass, sent_ref)


def square_kernel(x_ref, high_ref, low_ref):
    for start in range(0, x_ref.shape[0], ROW_STEP):
        span = slice(start, start + ROW_STEP)
        wide = x_ref[span, :].astype(F32)
        square = wide * wide
        high = square.astype(BF16)
        high_ref[span, :] = high
        low_ref[span, :] = (square - high.astype(F32)).astype(BF16)


def put_moments(both, x_ref, high_ref, low_ref, first_ref, second_ref, total_ref):
    part = first_ref.shape[0]
    first = dot_tn(both, x_ref[...])
    first_ref[...] = first[:part] + first[part:]
    second = dot_tn(both, high_ref[...])
    second_ref[...] = second[:part] + second[part:] + dot_tn(both[:, :part], low_ref[...])
    total = dot_tn(both, jnp.ones((both.shape[0], LANES), BF16))
    total_ref[...] = total[:part] + total[part:]


def split_parts(resp):
    high = resp.astype(BF16)
    low = (resp - high.astype(F32)).astype(BF16)
    return jnp.concatenate([high, low], axis=1)


def crossed_kernel(
    target, place_ref, got_ref, resp_ref, x_ref, high_ref, low_ref,
    kept_ref, first_ref, second_ref, total_ref, lent_ref,
):
    rows, comp = resp_ref.shape
    half = comp // 2
    y, z = place_ref[0] % 2, place_ref[0] // 2
    pull = target / get_mass(got_ref)
    left = lax.broadcasted_iota(jnp.int32, (ROW_STEP, half), 1) < half // 2
    for start in range(0, rows, ROW_STEP):
        span = slice(start, start + ROW_STEP)
        resp = balance_step(resp_ref[span, :], pull)
        same = jnp.where(z == 0, resp[:, :half], resp[:, half:])
        other = jnp.where(z == 0, resp[:, half:], resp[:, :half])
        same_turned = pltpu.roll(same, half // 2, 1)
        other_turned = pltpu.roll(other, half // 2, 1)
        lower = jnp.where(left, same, other_turned)
        upper = jnp.where(left, same_turned, other)
        kept_ref[span, :] = split_parts(jnp.where(y == 0, lower, upper))
        lent_ref[span, :] = split_parts(jnp.where(y == 0, upper, lower))
    put_moments(lent_ref[...], x_ref, high_ref, low_ref, first_ref, second_ref, total_ref)


def kept_kernel(kept_ref, x_ref, high_ref, low_ref, first_ref, second_ref, total_ref):
    put_moments(kept_ref[...], x_ref, high_ref, low_ref, first_ref, second_ref, total_ref)


def weights(mean_block, var_block):
    prec = 1.0 / var_block.astype(F32)
    mean_wide = mean_block.astype(F32)
    quad = (-0.5 * prec).astype(BF16)
    linear = (mean_wide * prec).astype(BF16)
    offset = -0.5 * jnp.sum(
        jnp.log(var_block.astype(F32)) + mean_wide * mean_wide * prec, axis=1
    )
    return quad, linear, offset[None, :]


def with_total(first, second, total):
    high = lax.reduce_precision(total, 5, 10)
    lane = lax.broadcasted_iota(jnp.int32, total.shape, 1)
    tail = jnp.where(lane < LANES // 2, high, total - high)
    return jnp.concatenate([first, second, tail], axis=1).astype(jnp.float16)


def split_total(payload, part):
    total = payload[:, 2 * part : 2 * part + 1] + payload[:, 2 * part + LANES // 2 :][:, :1]
    return payload[:, :part], payload[:, part : 2 * part], total


def on_device(embed, dest, means, variances):
    rows_dev, width = embed.shape
    groups = lax.axis_size("narrow")
    members = lax.axis_size("wide")
    block = rows_dev // groups
    comp = means.shape[0]
    half = comp // 2
    quarter = comp // 4
    deep = members // 4
    lines = [[4 * z + i for z in range(deep)] for i in range(4)]
    place = lax.axis_index("wide") % 4
    y, z = place % 2, place // 2
    scale = width ** (-0.5)
    target = float(rows_dev * members / comp)
    big = rows_dev * width
    area = rows_dev * comp

    everyone = functools.partial(
        lax.all_to_all, axis_name="wide", split_axis=0, concat_axis=0, tiled=True
    )
    resp_shape = jax.ShapeDtypeStruct((rows_dev, comp), F32)
    sent_shape = jax.ShapeDtypeStruct((members, comp // LANES, LANES), F32)

    ordered = call(
        functools.partial(order_kernel, groups),
        jax.ShapeDtypeStruct(embed.shape, BF16), 2, 2 * rows_dev * big, 4 * big,
    )(dest.reshape(1, rows_dev), embed)
    mine = lax.all_to_all(
        ordered.reshape(groups, block, width), "narrow", split_axis=0, concat_axis=0, tiled=True
    ).reshape(rows_dev, width)
    quad, linear, offset = weights(means, variances)
    resp, sent = call(
        functools.partial(score_kernel, scale), (resp_shape, sent_shape),
        4, 4 * big * comp, 2 * big + 4 * area,
    )(mine, quad, linear, offset)
    got = everyone(sent)
    for step in range(SINK - 1):
        resp, sent = call(
            functools.partial(balance_kernel, target), (resp_shape, sent_shape),
            2, 4 * area, 8 * area,
        )(got, resp)
        got = everyone(sent)
    plain = jax.ShapeDtypeStruct((rows_dev, width), BF16)
    high, low = call(square_kernel, (plain, plain), 1, 4 * big, 6 * big)(mine)
    sums = (
        jax.ShapeDtypeStruct((half, width), F32),
        jax.ShapeDtypeStruct((half, width), F32),
        jax.ShapeDtypeStruct((half, LANES), F32),
    )
    slab = jax.ShapeDtypeStruct((rows_dev, comp), BF16)
    kept, *lent = call(
        functools.partial(crossed_kernel, target), (slab, *sums), 5, 5 * big * comp,
        6 * big + 8 * area, scalars=1, scratch=[pltpu.VMEM((rows_dev, comp), BF16)],
    )(place.astype(jnp.int32).reshape(1), got, resp, mine, high, low)

    def to_partner(values, flip):
        return lax.ppermute(values, "wide", [(i, i ^ flip) for i in range(members)])

    sent = with_total(*lent)
    there = [to_partner(sent[:quarter], 1), to_partner(sent[quarter:], 3)]
    here = call(kept_kernel, sums, 4, 5 * big * comp, 6 * big + 2 * area)(kept, mine, high, low)
    there.append(to_partner(with_total(*(h[quarter:] for h in here)), 2))
    first, second, total = (h[:quarter] for h in here)
    for got in there:
        more = split_total(got.astype(F32), width)
        first, second, total = first + more[0], second + more[1], total + more[2]
    sent = with_total(SAFE * first, SAFE * second, SAFE * total)
    got = everyone(sent.reshape(deep, quarter // deep, sent.shape[1]), axis_index_groups=lines)
    first, second, total = split_total(jnp.sum(got.astype(F32), axis=0), width)
    new_mean = first / total
    new_var = second / total - new_mean * new_mean + 0.01
    done = jnp.concatenate([new_mean, new_var], axis=1).astype(jnp.float16)
    got = everyone(jnp.broadcast_to(done[None], (deep,) + done.shape), axis_index_groups=lines)
    here = got.reshape(quarter, 2 * width)
    by = [here] + [to_partner(here, flip) for flip in (1, 2, 3)]
    near = [jnp.where(y == 0, by[0], by[1]), jnp.where(y == 0, by[1], by[0])]
    far = [jnp.where(y == 0, by[2], by[3]), jnp.where(y == 0, by[3], by[2])]
    low = [jnp.where(z == 0, a, b) for a, b in zip(near, far)]
    high = [jnp.where(z == 0, b, a) for a, b in zip(near, far)]
    out = jnp.concatenate(low + high, axis=0).astype(F32)
    return (out[:, :width], out[:, width:])


def solution(mesh):
    return jax.shard_map(
        on_device,
        mesh=mesh,
        in_specs=(
            P(("wide", "narrow"), None),
            P(("wide", "narrow")),
            P("narrow", None),
            P("narrow", None),
        ),
        out_specs=(P("narrow", None), P("narrow", None)),
        check_vma=False,
    )
```

```python
import functools

import jax
import jax.numpy as jnp
from jax import lax
from jax.experimental import pallas as pl
from jax.experimental.pallas import tpu as pltpu
from jax.sharding import PartitionSpec as P

SINK = 3
LANES = 128
ROW_STEP = 256
SAFE = 0.25
F32 = jnp.float32
BF16 = jnp.bfloat16
VMEM_LIMIT = 24 * 1024 * 1024
ALL_VMEM = 60 * 1024 * 1024


def call(
    kernel, out_shape, n_in, flops, moved, scalars=0, remote=0, scratch=(), room=VMEM_LIMIT
):
    smem = pl.BlockSpec(memory_space=pltpu.SMEM)
    vmem = pl.BlockSpec(memory_space=pltpu.VMEM)
    hbm = pl.BlockSpec(memory_space=pltpu.HBM)
    return pl.pallas_call(
        kernel,
        out_shape=out_shape,
        in_specs=[smem] * scalars + [vmem] * n_in + [hbm] * remote,
        out_specs=jax.tree.map(lambda _: vmem, out_shape),
        scratch_shapes=scratch,
        compiler_params=pltpu.CompilerParams(vmem_limit_bytes=room),
        cost_estimate=pl.CostEstimate(flops=flops, bytes_accessed=moved, transcendentals=0),
    )


def dot_nt(a, b):
    return lax.dot_general(a, b, (((1,), (1,)), ((), ())), preferred_element_type=F32)


def dot_tn(a, b):
    return lax.dot_general(a, b, (((0,), (0,)), ((), ())), preferred_element_type=F32)


def order_kernel(groups, dest_ref, embed_hbm, out_ref, embed_ref, arrival):
    rows = embed_ref.shape[0]
    load = pltpu.make_async_copy(embed_hbm, embed_ref, arrival)
    load.start()
    block = rows // groups
    before = lax.broadcasted_iota(jnp.int32, (LANES, LANES), 0)
    after = lax.broadcasted_iota(jnp.int32, (LANES, LANES), 1)
    earlier = jnp.where(before < after, 1.0, 0.0).astype(BF16)
    group = lax.broadcasted_iota(jnp.int32, (groups, LANES), 0)
    base = (group * block).astype(F32)
    count = jnp.zeros((groups, 1), F32)
    places = []
    for start in range(0, rows, LANES):
        hot = jnp.where(group == dest_ref[:, start : start + LANES], 1.0, 0.0)
        rank = jnp.dot(hot.astype(BF16), earlier, preferred_element_type=F32) + count
        places.append(jnp.sum(hot * (rank + base), axis=0, keepdims=True))
        count = count + jnp.sum(hot, axis=1, keepdims=True)
    place = jnp.concatenate(places, axis=1).astype(jnp.int32)
    load.wait()
    for start in range(0, rows, ROW_STEP):
        slot = lax.broadcasted_iota(jnp.int32, (ROW_STEP, rows), 0) + start
        pick = jnp.where(slot == place, 1.0, 0.0).astype(BF16)
        got = jnp.dot(pick, embed_ref[...], preferred_element_type=F32)
        out_ref[start : start + ROW_STEP, :] = got.astype(BF16)


def put_mass(mass, sent_ref):
    for i in range(sent_ref.shape[1]):
        part = mass[:, i * LANES : (i + 1) * LANES]
        sent_ref[:, i, :] = jnp.broadcast_to(part, (sent_ref.shape[0], LANES))


def get_mass(got_ref):
    block = jnp.sum(got_ref[...], axis=0)
    return jnp.concatenate([block[i : i + 1] for i in range(block.shape[0])], axis=1)


def score_kernel(
    scale, x_ref, quad_ref, lin_ref, off_ref, resp_ref, high_ref, low_ref, sent_ref
):
    rows = x_ref.shape[0]
    mass = jnp.zeros((1, resp_ref.shape[1]), F32)
    for start in range(0, rows, ROW_STEP):
        span = slice(start, start + ROW_STEP)
        x = x_ref[span, :]
        wide = x.astype(F32)
        square = wide * wide
        high = square.astype(BF16)
        high_ref[span, :] = high
        low_ref[span, :] = (square - high.astype(F32)).astype(BF16)
        raw = dot_nt(high, quad_ref[...]) + dot_nt(x, lin_ref[...])
        score = scale * (raw + off_ref[...])
        lifted = jnp.exp(score - jnp.max(score, axis=1, keepdims=True))
        resp = lifted / jnp.sum(lifted, axis=1, keepdims=True)
        resp_ref[span, :] = resp
        mass = mass + jnp.sum(resp, axis=0, keepdims=True)
    put_mass(mass, sent_ref)


def balance_step(resp, pull):
    scaled = resp * pull
    return scaled / jnp.sum(scaled, axis=1, keepdims=True)


def balance_kernel(target, got_ref, resp_ref, out_ref, sent_ref):
    rows, comp = resp_ref.shape
    pull = target / get_mass(got_ref)
    mass = jnp.zeros((1, comp), F32)
    for start in range(0, rows, ROW_STEP):
        span = slice(start, start + ROW_STEP)
        resp = balance_step(resp_ref[span, :], pull)
        out_ref[span, :] = resp
        mass = mass + jnp.sum(resp, axis=0, keepdims=True)
    put_mass(mass, sent_ref)


def total_parts(total):
    coarse = jnp.floor(total / 8)
    rest = total - 8 * coarse
    middle = jnp.floor(rest * 2**6)
    rest = (rest - middle / 2**6) * 2**15
    fine = jnp.floor(rest)
    lane = lax.broadcasted_iota(jnp.int32, total.shape, 1)
    return jnp.where(
        lane < 64,
        jnp.where(lane < 32, coarse, middle),
        jnp.where(lane < 96, fine, rest - fine),
    )


def put_moments(both, x_ref, high_ref, low_ref, out_ref):
    part = out_ref.shape[0]
    width = x_ref.shape[1]
    first = dot_tn(both, x_ref[...])
    out_ref[:, :width] = first[:part] + first[part:]
    second = dot_tn(both, high_ref[...])
    out_ref[:, width : 2 * width] = (
        second[:part] + second[part:] + dot_tn(both[:, :part], low_ref[...])
    )
    total = dot_tn(both, jnp.ones((both.shape[0], LANES), BF16))
    out_ref[:, 2 * width :] = total_parts(total[:part] + total[part:])


def split_parts(resp):
    high = resp.astype(BF16)
    low = (resp - high.astype(F32)).astype(BF16)
    return jnp.concatenate([high, low], axis=1)


def crossed_kernel(
    target, place_ref, got_ref, resp_ref, x_ref, high_ref, low_ref,
    kept_ref, out_ref, lent_ref,
):
    rows, comp = resp_ref.shape
    half = comp // 2
    y, z = place_ref[0] % 2, place_ref[0] // 2
    pull = target / get_mass(got_ref)
    left = lax.broadcasted_iota(jnp.int32, (ROW_STEP, half), 1) < half // 2
    for start in range(0, rows, ROW_STEP):
        span = slice(start, start + ROW_STEP)
        resp = balance_step(resp_ref[span, :], pull)
        same = jnp.where(z == 0, resp[:, :half], resp[:, half:])
        other = jnp.where(z == 0, resp[:, half:], resp[:, :half])
        same_turned = pltpu.roll(same, half // 2, 1)
        other_turned = pltpu.roll(other, half // 2, 1)
        lower = jnp.where(left, same, other_turned)
        upper = jnp.where(left, same_turned, other)
        kept_ref[span, :] = split_parts(jnp.where(y == 0, lower, upper))
        lent_ref[span, :] = split_parts(jnp.where(y == 0, upper, lower))
    put_moments(lent_ref[...], x_ref, high_ref, low_ref, out_ref)


def kept_kernel(kept_ref, x_ref, high_ref, low_ref, out_ref):
    put_moments(kept_ref[...], x_ref, high_ref, low_ref, out_ref)


def weights(mean_block, var_block):
    prec = 1.0 / var_block.astype(F32)
    mean_wide = mean_block.astype(F32)
    quad = (-0.5 * prec).astype(BF16)
    linear = (mean_wide * prec).astype(BF16)
    offset = -0.5 * jnp.sum(
        jnp.log(var_block.astype(F32)) + mean_wide * mean_wide * prec, axis=1
    )
    return quad, linear, offset[None, :]


def on_device(embed, dest, means, variances):
    rows_dev, width = embed.shape
    groups = lax.axis_size("narrow")
    members = lax.axis_size("wide")
    block = rows_dev // groups
    comp = means.shape[0]
    half = comp // 2
    quarter = comp // 4
    deep = members // 4
    lines = [[4 * z + i for z in range(deep)] for i in range(4)]
    blocks = [[4 * z + i for i in range(4)] for z in range(deep)]
    place = (lax.axis_index("wide") % 4).astype(jnp.int32).reshape(1)
    scale = width ** (-0.5)
    target = float(rows_dev * members / comp)
    big = rows_dev * width
    area = rows_dev * comp

    everyone = functools.partial(
        lax.all_to_all, axis_name="wide", split_axis=0, concat_axis=0, tiled=True
    )
    resp_shape = jax.ShapeDtypeStruct((rows_dev, comp), F32)
    sent_shape = jax.ShapeDtypeStruct((members, comp // LANES, LANES), F32)

    ordered = call(
        functools.partial(order_kernel, groups),
        jax.ShapeDtypeStruct(embed.shape, BF16), 1, 2 * rows_dev * big, 4 * big, remote=1,
        scratch=[pltpu.VMEM(embed.shape, BF16), pltpu.SemaphoreType.DMA], room=ALL_VMEM,
    )(dest.reshape(1, rows_dev), embed)
    mine = lax.all_to_all(
        ordered.reshape(groups, block, width), "narrow", split_axis=0, concat_axis=0, tiled=True
    ).reshape(rows_dev, width)
    mine, place = lax.optimization_barrier((mine, place))
    quad, linear, offset = weights(means, variances)
    plain = jax.ShapeDtypeStruct((rows_dev, width), BF16)
    resp, high, low, sent = call(
        functools.partial(score_kernel, scale), (resp_shape, plain, plain, sent_shape),
        4, 4 * big * comp, 6 * big + 4 * area,
    )(mine, quad, linear, offset)
    got = everyone(sent)
    for step in range(SINK - 1):
        resp, sent = call(
            functools.partial(balance_kernel, target), (resp_shape, sent_shape),
            2, 4 * area, 8 * area,
        )(got, resp)
        got = everyone(sent)
    sums = jax.ShapeDtypeStruct((half, 2 * width + LANES), F32)
    slab = jax.ShapeDtypeStruct((rows_dev, comp), BF16)
    kept, lent = call(
        functools.partial(crossed_kernel, target), (slab, sums), 5, 5 * big * comp,
        6 * big + 8 * area, scalars=1, scratch=[pltpu.VMEM((rows_dev, comp), BF16)],
    )(place, got, resp, mine, high, low)

    def to_partner(values, flip):
        swap = [(i, i ^ flip) for i in range(members)]
        return lax.ppermute(values.astype(jnp.float16), "wide", swap).astype(F32)

    there = to_partner(lent[quarter:], 3), to_partner(lent[:quarter], 1)
    here = call(kept_kernel, sums, 4, 5 * big * comp, 6 * big + 2 * area)(kept, mine, high, low)
    near = to_partner(here[quarter:], 2)
    sent = (SAFE * (here[:quarter] + near + there[0] + there[1])).astype(jnp.float16)
    got = everyone(sent.reshape(deep, quarter // deep, sent.shape[1]), axis_index_groups=lines)
    got = jnp.sum(got.astype(F32), axis=0)
    first, second = got[:, :width], got[:, width : 2 * width]
    units = (8.0, 2.0**-6, 2.0**-15, 2.0**-15)
    total = sum(u * got[:, 2 * width + 32 * i :][:, :1] for i, u in enumerate(units))
    new_mean = first / total
    new_var = second / total - new_mean * new_mean + 0.01
    done = jnp.concatenate([new_mean, new_var], axis=1).astype(jnp.float16)
    got = everyone(jnp.broadcast_to(done[None], (deep,) + done.shape), axis_index_groups=lines)
    here = got.reshape(1, quarter, 2 * width)
    got = everyone(jnp.broadcast_to(here, (4,) + here.shape[1:]), axis_index_groups=blocks)
    out = got.reshape(comp, 2 * width).astype(F32)
    return (out[:, :width], out[:, width:])


def solution(mesh):
    return jax.shard_map(
        on_device,
        mesh=mesh,
        in_specs=(
            P(("wide", "narrow"), None),
            P(("wide", "narrow")),
            P("narrow", None),
            P("narrow", None),
        ),
        out_specs=(P("narrow", None), P("narrow", None)),
        check_vma=False,
    )
```

```python
import functools

import jax
import jax.numpy as jnp
from jax import lax
from jax.experimental import pallas as pl
from jax.experimental.pallas import tpu as pltpu
from jax.sharding import PartitionSpec as P

SINK = 3
LANES = 128
ROW_STEP = 256
SAFE = 0.25
F32 = jnp.float32
BF16 = jnp.bfloat16
VMEM_LIMIT = 24 * 1024 * 1024


def call(kernel, out_shape, n_in, flops, moved, remote=0, scratch=()):
    vmem = pl.BlockSpec(memory_space=pltpu.VMEM)
    hbm = pl.BlockSpec(memory_space=pltpu.HBM)
    return pl.pallas_call(
        kernel,
        out_shape=out_shape,
        in_specs=[vmem] * n_in + [hbm] * remote,
        out_specs=jax.tree.map(lambda _: vmem, out_shape),
        scratch_shapes=scratch,
        compiler_params=pltpu.CompilerParams(vmem_limit_bytes=VMEM_LIMIT),
        cost_estimate=pl.CostEstimate(flops=flops, bytes_accessed=moved, transcendentals=0),
    )


def dot_nt(a, b):
    return lax.dot_general(a, b, (((1,), (1,)), ((), ())), preferred_element_type=F32)


def dot_tn(a, b):
    return lax.dot_general(a, b, (((0,), (0,)), ((), ())), preferred_element_type=F32)


def prepare_kernel(
    groups, dest_hbm, var_hbm, mean_hbm, embed_hbm, out_ref, quad_ref, lin_ref, off_ref,
    dest_ref, var_ref, mean_ref, embed_ref, arrivals,
):
    rows, width = embed_ref.shape
    comp = mean_ref.shape[0]
    block = rows // groups
    spans = [slice(start, start + ROW_STEP) for start in range(0, rows, ROW_STEP)]
    pairs = [(dest_hbm, dest_ref), (var_hbm, var_ref), (mean_hbm, mean_ref)]
    pairs += [(embed_hbm.at[span], embed_ref.at[span]) for span in spans]
    loads = [pltpu.make_async_copy(*pair, arrivals.at[i]) for i, pair in enumerate(pairs)]
    for load in loads:
        load.start()
    loads[0].wait()
    before = lax.broadcasted_iota(jnp.int32, (LANES, LANES), 0)
    after = lax.broadcasted_iota(jnp.int32, (LANES, LANES), 1)
    earlier = jnp.where(before < after, 1.0, 0.0).astype(BF16)
    group = lax.broadcasted_iota(jnp.int32, (groups, LANES), 0)
    base = (group * block).astype(F32)
    count = jnp.zeros((groups, 1), F32)
    places = []
    for start in range(0, rows, LANES):
        hot = jnp.where(group == dest_ref[start : start + LANES][None, :], 1.0, 0.0)
        rank = jnp.dot(hot.astype(BF16), earlier, preferred_element_type=F32) + count
        places.append(jnp.sum(hot * (rank + base), axis=0, keepdims=True))
        count = count + jnp.sum(hot, axis=1, keepdims=True)
    place = jnp.concatenate(places, axis=1).astype(jnp.int32)
    loads[1].wait()
    loads[2].wait()
    offsets = []
    for start in range(0, comp, LANES):
        span = slice(start, start + LANES)
        var = var_ref[span, :].astype(F32)
        mean = mean_ref[span, :].astype(F32)
        prec = 1.0 / var
        scaled = mean * prec
        quad_ref[span, :] = (-0.5 * prec).astype(BF16)
        lin_ref[span, :] = scaled.astype(BF16)
        term = jnp.log(var) + mean * scaled
        part = sum(term[:, i : i + LANES] for i in range(0, width, LANES))
        offsets.append(-0.5 * jnp.sum(jnp.transpose(part), axis=0, keepdims=True))
    off_ref[...] = jnp.concatenate(offsets, axis=1)
    for load in loads[3:]:
        load.wait()
    for span in spans:
        slot = lax.broadcasted_iota(jnp.int32, (ROW_STEP, rows), 0) + span.start
        pick = jnp.where(slot == place, 1.0, 0.0).astype(BF16)
        got = jnp.dot(pick, embed_ref[...], preferred_element_type=F32)
        out_ref[span, :] = got.astype(BF16)


def put_mass(mass, sent_ref):
    for i in range(sent_ref.shape[1]):
        part = mass[:, i * LANES : (i + 1) * LANES]
        sent_ref[:, i, :] = jnp.broadcast_to(part, (sent_ref.shape[0], LANES))


def get_mass(got_ref):
    block = jnp.sum(got_ref[...], axis=0)
    return jnp.concatenate([block[i : i + 1] for i in range(block.shape[0])], axis=1)


def score_kernel(
    scale, x_ref, quad_ref, lin_ref, off_ref, resp_ref, high_ref, low_ref, sent_ref
):
    rows = x_ref.shape[0]
    mass = jnp.zeros((1, resp_ref.shape[1]), F32)
    for start in range(0, rows, ROW_STEP):
        span = slice(start, start + ROW_STEP)
        x = x_ref[span, :]
        wide = x.astype(F32)
        square = wide * wide
        high = square.astype(BF16)
        high_ref[span, :] = high
        low_ref[span, :] = (square - high.astype(F32)).astype(BF16)
        raw = dot_nt(high, quad_ref[...]) + dot_nt(x, lin_ref[...])
        score = scale * (raw + off_ref[...])
        lifted = jnp.exp(score - jnp.max(score, axis=1, keepdims=True))
        resp = lifted / jnp.sum(lifted, axis=1, keepdims=True)
        resp_ref[span, :] = resp
        mass = mass + jnp.sum(resp, axis=0, keepdims=True)
    put_mass(mass, sent_ref)


def balance_step(resp, pull):
    scaled = resp * pull
    return scaled / jnp.sum(scaled, axis=1, keepdims=True)


def balance_kernel(target, got_ref, resp_ref, out_ref, sent_ref):
    rows, comp = resp_ref.shape
    pull = target / get_mass(got_ref)
    mass = jnp.zeros((1, comp), F32)
    for start in range(0, rows, ROW_STEP):
        span = slice(start, start + ROW_STEP)
        resp = balance_step(resp_ref[span, :], pull)
        out_ref[span, :] = resp
        mass = mass + jnp.sum(resp, axis=0, keepdims=True)
    put_mass(mass, sent_ref)


def total_parts(total):
    coarse = jnp.floor(total / 8)
    rest = total - 8 * coarse
    middle = jnp.floor(rest * 2**6)
    rest = (rest - middle / 2**6) * 2**15
    fine = jnp.floor(rest)
    lane = lax.broadcasted_iota(jnp.int32, total.shape, 1)
    return jnp.where(
        lane < 64,
        jnp.where(lane < 32, coarse, middle),
        jnp.where(lane < 96, fine, rest - fine),
    )


def put_moments(both, x_ref, high_ref, low_ref, out_ref):
    part = out_ref.shape[0]
    width = x_ref.shape[1]
    first = dot_tn(both, x_ref[...])
    out_ref[:, :width] = first[:part] + first[part:]
    second = dot_tn(both, high_ref[...])
    out_ref[:, width : 2 * width] = (
        second[:part] + second[part:] + dot_tn(both[:, :part], low_ref[...])
    )
    total = dot_tn(both, jnp.ones((both.shape[0], LANES), BF16))
    out_ref[:, 2 * width :] = total_parts(total[:part] + total[part:])


def moment_kernel(
    target, got_ref, resp_ref, x_ref, high_ref, low_ref, out_ref, both_ref
):
    rows, comp = resp_ref.shape
    pull = target / get_mass(got_ref)
    for start in range(0, rows, ROW_STEP):
        span = slice(start, start + ROW_STEP)
        resp = balance_step(resp_ref[span, :], pull)
        high = resp.astype(BF16)
        both_ref[span, :comp] = high
        both_ref[span, comp:] = (resp - high.astype(F32)).astype(BF16)
    put_moments(both_ref[...], x_ref, high_ref, low_ref, out_ref)


def on_device(embed, dest, means, variances):
    rows_dev, width = embed.shape
    groups = lax.axis_size("narrow")
    members = lax.axis_size("wide")
    block = rows_dev // groups
    comp = means.shape[0]
    quarter = comp // 4
    deep = members // 4
    lines = [[4 * z + i for z in range(deep)] for i in range(4)]
    blocks = [[4 * z + i for i in range(4)] for z in range(deep)]
    scale = width ** (-0.5)
    target = float(rows_dev * members / comp)
    big = rows_dev * width
    area = rows_dev * comp

    everyone = functools.partial(
        lax.all_to_all, axis_name="wide", split_axis=0, concat_axis=0, tiled=True
    )
    resp_shape = jax.ShapeDtypeStruct((rows_dev, comp), F32)
    sent_shape = jax.ShapeDtypeStruct((members, comp // LANES, LANES), F32)

    plain = jax.ShapeDtypeStruct((rows_dev, width), BF16)
    weight = jax.ShapeDtypeStruct((comp, width), BF16)
    ordered, quad, linear, offset = call(
        functools.partial(prepare_kernel, groups),
        (plain, weight, weight, jax.ShapeDtypeStruct((1, comp), F32)),
        0, 2 * rows_dev * big, 4 * big, remote=4,
        scratch=[
            pltpu.VMEM(dest.shape, jnp.int32),
            pltpu.VMEM(variances.shape, BF16),
            pltpu.VMEM(means.shape, BF16),
            pltpu.VMEM(embed.shape, BF16),
            pltpu.SemaphoreType.DMA((3 + rows_dev // ROW_STEP,)),
        ],
    )(*(pltpu.with_memory_space_constraint(a, pltpu.HBM) for a in (dest, variances, means, embed)))
    mine = lax.all_to_all(
        ordered.reshape(groups, block, width), "narrow", split_axis=0, concat_axis=0, tiled=True
    ).reshape(rows_dev, width)
    resp, high, low, sent = call(
        functools.partial(score_kernel, scale), (resp_shape, plain, plain, sent_shape),
        4, 4 * big * comp, 6 * big + 4 * area,
    )(mine, quad, linear, offset)
    got = everyone(sent)
    for step in range(SINK - 1):
        resp, sent = call(
            functools.partial(balance_kernel, target), (resp_shape, sent_shape),
            2, 4 * area, 8 * area,
        )(got, resp)
        got = everyone(sent)
    sums = call(
        functools.partial(moment_kernel, target),
        jax.ShapeDtypeStruct((comp, 2 * width + LANES), F32), 5, 10 * big * comp,
        6 * big + 8 * area, scratch=[pltpu.VMEM((rows_dev, 2 * comp), BF16)],
    )(got, resp, mine, high, low)
    sent = sums.astype(jnp.float16).reshape(4, quarter, sums.shape[1])
    got = everyone(sent, axis_index_groups=blocks)
    sent = (SAFE * jnp.sum(got.astype(F32), axis=0)).astype(jnp.float16)
    got = everyone(sent.reshape(deep, quarter // deep, sent.shape[1]), axis_index_groups=lines)
    got = jnp.sum(got.astype(F32), axis=0)
    first, second = got[:, :width], got[:, width : 2 * width]
    units = (8.0, 2.0**-6, 2.0**-15, 2.0**-15)
    total = sum(u * got[:, 2 * width + 32 * i :][:, :1] for i, u in enumerate(units))
    new_mean = first / total
    new_var = second / total - new_mean * new_mean + 0.01
    done = jnp.concatenate([new_mean, new_var], axis=1).astype(jnp.float16)
    got = everyone(jnp.broadcast_to(done[None], (deep,) + done.shape), axis_index_groups=lines)
    here = got.reshape(1, quarter, 2 * width)
    got = everyone(jnp.broadcast_to(here, (4,) + here.shape[1:]), axis_index_groups=blocks)
    out = got.reshape(comp, 2 * width).astype(F32)
    return (out[:, :width], out[:, width:])


def solution(mesh):
    return jax.shard_map(
        on_device,
        mesh=mesh,
        in_specs=(
            P(("wide", "narrow"), None),
            P(("wide", "narrow")),
            P("narrow", None),
            P("narrow", None),
        ),
        out_specs=(P("narrow", None), P("narrow", None)),
        check_vma=False,
    )
```

```python
import functools

import jax
import jax.numpy as jnp
from jax import lax
from jax.experimental import pallas as pl
from jax.experimental.pallas import tpu as pltpu
from jax.sharding import PartitionSpec as P

SINK = 3
LANES = 128
ROW_STEP = 256
SAFE = 0.25
F32 = jnp.float32
BF16 = jnp.bfloat16
VMEM_LIMIT = 24 * 1024 * 1024


def call(kernel, out_shape, n_in, flops, moved, remote=0, scratch=()):
    vmem = pl.BlockSpec(memory_space=pltpu.VMEM)
    hbm = pl.BlockSpec(memory_space=pltpu.HBM)
    return pl.pallas_call(
        kernel,
        out_shape=out_shape,
        in_specs=[vmem] * n_in + [hbm] * remote,
        out_specs=jax.tree.map(lambda _: vmem, out_shape),
        scratch_shapes=scratch,
        compiler_params=pltpu.CompilerParams(vmem_limit_bytes=VMEM_LIMIT),
        cost_estimate=pl.CostEstimate(flops=flops, bytes_accessed=moved, transcendentals=0),
    )


def in_hbm(array):
    return pltpu.with_memory_space_constraint(array, pltpu.HBM)


def dot_nt(a, b):
    return lax.dot_general(a, b, (((1,), (1,)), ((), ())), preferred_element_type=F32)


def dot_tn(a, b):
    return lax.dot_general(a, b, (((0,), (0,)), ((), ())), preferred_element_type=F32)


def order_kernel(groups, dest_hbm, embed_hbm, out_ref, dest_ref, embed_ref, arrivals):
    rows = embed_ref.shape[0]
    block = rows // groups
    spans = [slice(start, start + ROW_STEP) for start in range(0, rows, ROW_STEP)]
    pairs = [(dest_hbm, dest_ref)]
    pairs += [(embed_hbm.at[span], embed_ref.at[span]) for span in spans]
    loads = [pltpu.make_async_copy(*pair, arrivals.at[i]) for i, pair in enumerate(pairs)]
    for load in loads:
        load.start()
    loads[0].wait()
    before = lax.broadcasted_iota(jnp.int32, (LANES, LANES), 0)
    after = lax.broadcasted_iota(jnp.int32, (LANES, LANES), 1)
    earlier = jnp.where(before < after, 1.0, 0.0).astype(BF16)
    group = lax.broadcasted_iota(jnp.int32, (groups, LANES), 0)
    base = (group * block).astype(F32)
    count = jnp.zeros((groups, 1), F32)
    places = []
    for start in range(0, rows, LANES):
        hot = jnp.where(group == dest_ref[start : start + LANES][None, :], 1.0, 0.0)
        rank = jnp.dot(hot.astype(BF16), earlier, preferred_element_type=F32) + count
        places.append(jnp.sum(hot * (rank + base), axis=0, keepdims=True))
        count = count + jnp.sum(hot, axis=1, keepdims=True)
    place = jnp.concatenate(places, axis=1).astype(jnp.int32)
    for load in loads[1:]:
        load.wait()
    for span in spans:
        slot = lax.broadcasted_iota(jnp.int32, (ROW_STEP, rows), 0) + span.start
        pick = jnp.where(slot == place, 1.0, 0.0).astype(BF16)
        got = jnp.dot(pick, embed_ref[...], preferred_element_type=F32)
        out_ref[span, :] = got.astype(BF16)


def weight_kernel(
    var_hbm, mean_hbm, quad_ref, lin_ref, off_ref, var_ref, mean_ref, arrivals
):
    comp, width = mean_ref.shape
    pairs = [(var_hbm, var_ref), (mean_hbm, mean_ref)]
    loads = [pltpu.make_async_copy(*pair, arrivals.at[i]) for i, pair in enumerate(pairs)]
    for load in loads:
        load.start()
    for load in loads:
        load.wait()
    offsets = []
    for start in range(0, comp, LANES):
        span = slice(start, start + LANES)
        var = var_ref[span, :].astype(F32)
        mean = mean_ref[span, :].astype(F32)
        prec = 1.0 / var
        scaled = mean * prec
        quad_ref[span, :] = (-0.5 * prec).astype(BF16)
        lin_ref[span, :] = scaled.astype(BF16)
        term = jnp.log(var) + mean * scaled
        part = sum(term[:, i : i + LANES] for i in range(0, width, LANES))
        offsets.append(-0.5 * jnp.sum(jnp.transpose(part), axis=0, keepdims=True))
    off_ref[...] = jnp.concatenate(offsets, axis=1)


def put_mass(mass, sent_ref):
    for i in range(sent_ref.shape[1]):
        part = mass[:, i * LANES : (i + 1) * LANES]
        sent_ref[:, i, :] = jnp.broadcast_to(part, (sent_ref.shape[0], LANES))


def get_mass(got_ref):
    block = jnp.sum(got_ref[...], axis=0)
    return jnp.concatenate([block[i : i + 1] for i in range(block.shape[0])], axis=1)


def score_kernel(
    scale, x_ref, quad_ref, lin_ref, off_ref, resp_ref, high_ref, low_ref, sent_ref
):
    rows = x_ref.shape[0]
    mass = jnp.zeros((1, resp_ref.shape[1]), F32)
    for start in range(0, rows, ROW_STEP):
        span = slice(start, start + ROW_STEP)
        x = x_ref[span, :]
        wide = x.astype(F32)
        square = wide * wide
        high = square.astype(BF16)
        high_ref[span, :] = high
        low_ref[span, :] = (square - high.astype(F32)).astype(BF16)
        raw = dot_nt(high, quad_ref[...]) + dot_nt(x, lin_ref[...])
        score = scale * (raw + off_ref[...])
        lifted = jnp.exp(score - jnp.max(score, axis=1, keepdims=True))
        resp = lifted / jnp.sum(lifted, axis=1, keepdims=True)
        resp_ref[span, :] = resp
        mass = mass + jnp.sum(resp, axis=0, keepdims=True)
    put_mass(mass, sent_ref)


def balance_step(resp, pull):
    scaled = resp * pull
    return scaled / jnp.sum(scaled, axis=1, keepdims=True)


def balance_kernel(target, got_ref, resp_ref, out_ref, sent_ref):
    rows, comp = resp_ref.shape
    pull = target / get_mass(got_ref)
    mass = jnp.zeros((1, comp), F32)
    for start in range(0, rows, ROW_STEP):
        span = slice(start, start + ROW_STEP)
        resp = balance_step(resp_ref[span, :], pull)
        out_ref[span, :] = resp
        mass = mass + jnp.sum(resp, axis=0, keepdims=True)
    put_mass(mass, sent_ref)


def total_parts(total):
    coarse = jnp.floor(total / 8)
    rest = total - 8 * coarse
    middle = jnp.floor(rest * 2**6)
    rest = (rest - middle / 2**6) * 2**15
    fine = jnp.floor(rest)
    lane = lax.broadcasted_iota(jnp.int32, total.shape, 1)
    return jnp.where(
        lane < 64,
        jnp.where(lane < 32, coarse, middle),
        jnp.where(lane < 96, fine, rest - fine),
    )


def put_moments(both, x_ref, high_ref, low_ref, out_ref):
    part = out_ref.shape[0]
    width = x_ref.shape[1]
    first = dot_tn(both, x_ref[...])
    out_ref[:, :width] = first[:part] + first[part:]
    second = dot_tn(both, high_ref[...])
    out_ref[:, width : 2 * width] = (
        second[:part] + second[part:] + dot_tn(both[:, :part], low_ref[...])
    )
    total = dot_tn(both, jnp.ones((both.shape[0], LANES), BF16))
    out_ref[:, 2 * width :] = total_parts(total[:part] + total[part:])


def moment_kernel(
    target, got_ref, resp_ref, x_ref, high_ref, low_ref, out_ref, both_ref
):
    rows, comp = resp_ref.shape
    pull = target / get_mass(got_ref)
    for start in range(0, rows, ROW_STEP):
        span = slice(start, start + ROW_STEP)
        resp = balance_step(resp_ref[span, :], pull)
        high = resp.astype(BF16)
        both_ref[span, :comp] = high
        both_ref[span, comp:] = (resp - high.astype(F32)).astype(BF16)
    put_moments(both_ref[...], x_ref, high_ref, low_ref, out_ref)


def on_device(embed, dest, means, variances):
    rows_dev, width = embed.shape
    groups = lax.axis_size("narrow")
    members = lax.axis_size("wide")
    block = rows_dev // groups
    comp = means.shape[0]
    quarter = comp // 4
    deep = members // 4
    lines = [[4 * z + i for z in range(deep)] for i in range(4)]
    blocks = [[4 * z + i for i in range(4)] for z in range(deep)]
    scale = width ** (-0.5)
    target = float(rows_dev * members / comp)
    big = rows_dev * width
    area = rows_dev * comp

    everyone = functools.partial(
        lax.all_to_all, axis_name="wide", split_axis=0, concat_axis=0, tiled=True
    )
    resp_shape = jax.ShapeDtypeStruct((rows_dev, comp), F32)
    sent_shape = jax.ShapeDtypeStruct((members, comp // LANES, LANES), F32)

    plain = jax.ShapeDtypeStruct((rows_dev, width), BF16)
    weight = jax.ShapeDtypeStruct((comp, width), BF16)
    ordered = call(
        functools.partial(order_kernel, groups), plain, 0, 2 * rows_dev * big, 4 * big, remote=2,
        scratch=[
            pltpu.VMEM(dest.shape, jnp.int32),
            pltpu.VMEM(embed.shape, BF16),
            pltpu.SemaphoreType.DMA((1 + rows_dev // ROW_STEP,)),
        ],
    )(*(in_hbm(a) for a in (dest, embed)))
    quad, linear, offset = call(
        weight_kernel, (weight, weight, jax.ShapeDtypeStruct((1, comp), F32)),
        0, 8 * comp * width, 8 * comp * width, remote=2,
        scratch=[
            pltpu.VMEM(variances.shape, BF16),
            pltpu.VMEM(means.shape, BF16),
            pltpu.SemaphoreType.DMA((2,)),
        ],
    )(*(in_hbm(a) for a in (variances, means)))
    mine = lax.all_to_all(
        ordered.reshape(groups, block, width), "narrow", split_axis=0, concat_axis=0, tiled=True
    ).reshape(rows_dev, width)
    resp, high, low, sent = call(
        functools.partial(score_kernel, scale), (resp_shape, plain, plain, sent_shape),
        4, 4 * big * comp, 6 * big + 4 * area,
    )(mine, quad, linear, offset)
    got = everyone(sent)
    for step in range(SINK - 1):
        resp, sent = call(
            functools.partial(balance_kernel, target), (resp_shape, sent_shape),
            2, 4 * area, 8 * area,
        )(got, resp)
        got = everyone(sent)
    sums = call(
        functools.partial(moment_kernel, target),
        jax.ShapeDtypeStruct((comp, 2 * width + LANES), F32), 5, 10 * big * comp,
        6 * big + 8 * area, scratch=[pltpu.VMEM((rows_dev, 2 * comp), BF16)],
    )(got, resp, mine, high, low)
    sent = sums.astype(jnp.float16).reshape(4, quarter, sums.shape[1])
    got = everyone(sent, axis_index_groups=blocks)
    sent = (SAFE * jnp.sum(got.astype(F32), axis=0)).astype(jnp.float16)
    got = everyone(sent.reshape(deep, quarter // deep, sent.shape[1]), axis_index_groups=lines)
    got = jnp.sum(got.astype(F32), axis=0)
    first, second = got[:, :width], got[:, width : 2 * width]
    units = (8.0, 2.0**-6, 2.0**-15, 2.0**-15)
    total = sum(u * got[:, 2 * width + 32 * i :][:, :1] for i, u in enumerate(units))
    new_mean = first / total
    new_var = second / total - new_mean * new_mean + 0.01
    done = jnp.concatenate([new_mean, new_var], axis=1).astype(jnp.float16)
    got = everyone(jnp.broadcast_to(done[None], (deep,) + done.shape), axis_index_groups=lines)
    here = got.reshape(1, quarter, 2 * width)
    got = everyone(jnp.broadcast_to(here, (4,) + here.shape[1:]), axis_index_groups=blocks)
    out = lax.optimization_barrier(got.reshape(comp, 2 * width))
    return (out[:, :width].astype(F32), out[:, width:].astype(F32))


def solution(mesh):
    return jax.shard_map(
        on_device,
        mesh=mesh,
        in_specs=(
            P(("wide", "narrow"), None),
            P(("wide", "narrow")),
            P("narrow", None),
            P("narrow", None),
        ),
        out_specs=(P("narrow", None), P("narrow", None)),
        check_vma=False,
    )
```

```python
import functools

import jax
import jax.numpy as jnp
from jax import lax
from jax.experimental import pallas as pl
from jax.experimental.pallas import tpu as pltpu
from jax.sharding import PartitionSpec as P

SINK = 3
LANES = 128
ROW_STEP = 256
SAFE = 0.25
F32 = jnp.float32
BF16 = jnp.bfloat16
VMEM_LIMIT = 24 * 1024 * 1024


def call(
    kernel, out_shape, n_in, flops, moved, remote=0, scratch=(), out_space=pltpu.VMEM
):
    vmem = pl.BlockSpec(memory_space=pltpu.VMEM)
    hbm = pl.BlockSpec(memory_space=pltpu.HBM)
    return pl.pallas_call(
        kernel,
        out_shape=out_shape,
        in_specs=[vmem] * n_in + [hbm] * remote,
        out_specs=jax.tree.map(lambda _: pl.BlockSpec(memory_space=out_space), out_shape),
        scratch_shapes=scratch,
        compiler_params=pltpu.CompilerParams(vmem_limit_bytes=VMEM_LIMIT),
        cost_estimate=pl.CostEstimate(flops=flops, bytes_accessed=moved, transcendentals=0),
    )


def in_hbm(array):
    return pltpu.with_memory_space_constraint(array, pltpu.HBM)


def dot_nt(a, b):
    return lax.dot_general(a, b, (((1,), (1,)), ((), ())), preferred_element_type=F32)


def dot_tn(a, b):
    return lax.dot_general(a, b, (((0,), (0,)), ((), ())), preferred_element_type=F32)


def order_kernel(
    groups, dest_hbm, embed_hbm, out_hbm, dest_ref, embed_ref, out_ref, arrivals, departures
):
    rows = embed_ref.shape[0]
    block = rows // groups
    spans = [slice(start, start + ROW_STEP) for start in range(0, rows, ROW_STEP)]
    pairs = [(dest_hbm, dest_ref)]
    pairs += [(embed_hbm.at[span], embed_ref.at[span]) for span in spans]
    loads = [pltpu.make_async_copy(*pair, arrivals.at[i]) for i, pair in enumerate(pairs)]
    for load in loads:
        load.start()
    loads[0].wait()
    before = lax.broadcasted_iota(jnp.int32, (LANES, LANES), 0)
    after = lax.broadcasted_iota(jnp.int32, (LANES, LANES), 1)
    earlier = jnp.where(before < after, 1.0, 0.0).astype(BF16)
    group = lax.broadcasted_iota(jnp.int32, (groups, LANES), 0)
    base = (group * block).astype(F32)
    count = jnp.zeros((groups, 1), F32)
    places = []
    for start in range(0, rows, LANES):
        hot = jnp.where(group == dest_ref[start : start + LANES][None, :], 1.0, 0.0)
        rank = jnp.dot(hot.astype(BF16), earlier, preferred_element_type=F32) + count
        places.append(jnp.sum(hot * (rank + base), axis=0, keepdims=True))
        count = count + jnp.sum(hot, axis=1, keepdims=True)
    place = jnp.concatenate(places, axis=1).astype(jnp.int32)
    for load in loads[1:]:
        load.wait()
    stores = []
    for span in spans:
        slot = lax.broadcasted_iota(jnp.int32, (ROW_STEP, rows), 0) + span.start
        pick = jnp.where(slot == place, 1.0, 0.0).astype(BF16)
        got = jnp.dot(pick, embed_ref[...], preferred_element_type=F32)
        out_ref[span, :] = got.astype(BF16)
        stores.append(
            pltpu.make_async_copy(
                out_ref.at[span], out_hbm.at[span], departures.at[len(stores)]
            )
        )
        stores[-1].start()
    for store in stores:
        store.wait()


def weight_kernel(
    var_hbm, mean_hbm, quad_ref, lin_ref, off_ref, var_ref, mean_ref, arrivals
):
    comp, width = mean_ref.shape
    pairs = [(var_hbm, var_ref), (mean_hbm, mean_ref)]
    loads = [pltpu.make_async_copy(*pair, arrivals.at[i]) for i, pair in enumerate(pairs)]
    for load in loads:
        load.start()
    for load in loads:
        load.wait()
    offsets = []
    for start in range(0, comp, LANES):
        span = slice(start, start + LANES)
        var = var_ref[span, :].astype(F32)
        mean = mean_ref[span, :].astype(F32)
        prec = 1.0 / var
        scaled = mean * prec
        quad_ref[span, :] = (-0.5 * prec).astype(BF16)
        lin_ref[span, :] = scaled.astype(BF16)
        term = jnp.log(var) + mean * scaled
        part = sum(term[:, i : i + LANES] for i in range(0, width, LANES))
        offsets.append(-0.5 * jnp.sum(jnp.transpose(part), axis=0, keepdims=True))
    off_ref[...] = jnp.concatenate(offsets, axis=1)


def put_mass(mass, sent_ref):
    for i in range(sent_ref.shape[1]):
        part = mass[:, i * LANES : (i + 1) * LANES]
        sent_ref[:, i, :] = jnp.broadcast_to(part, (sent_ref.shape[0], LANES))


def get_mass(got_ref):
    block = jnp.sum(got_ref[...], axis=0)
    return jnp.concatenate([block[i : i + 1] for i in range(block.shape[0])], axis=1)


def score_kernel(
    scale, x_ref, quad_ref, lin_ref, off_ref, resp_ref, high_ref, low_ref, sent_ref
):
    rows = x_ref.shape[0]
    mass = jnp.zeros((1, resp_ref.shape[1]), F32)
    for start in range(0, rows, ROW_STEP):
        span = slice(start, start + ROW_STEP)
        x = x_ref[span, :]
        wide = x.astype(F32)
        square = wide * wide
        high = square.astype(BF16)
        high_ref[span, :] = high
        low_ref[span, :] = (square - high.astype(F32)).astype(BF16)
        raw = dot_nt(high, quad_ref[...]) + dot_nt(x, lin_ref[...])
        score = scale * (raw + off_ref[...])
        lifted = jnp.exp(score - jnp.max(score, axis=1, keepdims=True))
        resp = lifted / jnp.sum(lifted, axis=1, keepdims=True)
        resp_ref[span, :] = resp
        mass = mass + jnp.sum(resp, axis=0, keepdims=True)
    put_mass(mass, sent_ref)


def balance_step(resp, pull):
    scaled = resp * pull
    return scaled / jnp.sum(scaled, axis=1, keepdims=True)


def balance_kernel(target, got_ref, resp_ref, out_ref, sent_ref):
    rows, comp = resp_ref.shape
    pull = target / get_mass(got_ref)
    mass = jnp.zeros((1, comp), F32)
    for start in range(0, rows, ROW_STEP):
        span = slice(start, start + ROW_STEP)
        resp = balance_step(resp_ref[span, :], pull)
        out_ref[span, :] = resp
        mass = mass + jnp.sum(resp, axis=0, keepdims=True)
    put_mass(mass, sent_ref)


def total_parts(total):
    coarse = jnp.floor(total / 8)
    rest = total - 8 * coarse
    middle = jnp.floor(rest * 2**6)
    rest = (rest - middle / 2**6) * 2**15
    fine = jnp.floor(rest)
    lane = lax.broadcasted_iota(jnp.int32, total.shape, 1)
    return jnp.where(
        lane < 64,
        jnp.where(lane < 32, coarse, middle),
        jnp.where(lane < 96, fine, rest - fine),
    )


def put_moments(both, x_ref, high_ref, low_ref, out_ref):
    part = out_ref.shape[0]
    width = x_ref.shape[1]
    first = dot_tn(both, x_ref[...])
    out_ref[:, :width] = first[:part] + first[part:]
    second = dot_tn(both, high_ref[...])
    out_ref[:, width : 2 * width] = (
        second[:part] + second[part:] + dot_tn(both[:, :part], low_ref[...])
    )
    total = dot_tn(both, jnp.ones((both.shape[0], LANES), BF16))
    out_ref[:, 2 * width :] = total_parts(total[:part] + total[part:])


def moment_kernel(
    target, got_ref, resp_ref, x_ref, high_ref, low_ref, out_ref, both_ref
):
    rows, comp = resp_ref.shape
    pull = target / get_mass(got_ref)
    for start in range(0, rows, ROW_STEP):
        span = slice(start, start + ROW_STEP)
        resp = balance_step(resp_ref[span, :], pull)
        high = resp.astype(BF16)
        both_ref[span, :comp] = high
        both_ref[span, comp:] = (resp - high.astype(F32)).astype(BF16)
    put_moments(both_ref[...], x_ref, high_ref, low_ref, out_ref)


def on_device(embed, dest, means, variances):
    rows_dev, width = embed.shape
    groups = lax.axis_size("narrow")
    members = lax.axis_size("wide")
    block = rows_dev // groups
    comp = means.shape[0]
    quarter = comp // 4
    deep = members // 4
    lines = [[4 * z + i for z in range(deep)] for i in range(4)]
    blocks = [[4 * z + i for i in range(4)] for z in range(deep)]
    scale = width ** (-0.5)
    target = float(rows_dev * members / comp)
    big = rows_dev * width
    area = rows_dev * comp

    everyone = functools.partial(
        lax.all_to_all, axis_name="wide", split_axis=0, concat_axis=0, tiled=True
    )
    resp_shape = jax.ShapeDtypeStruct((rows_dev, comp), F32)
    sent_shape = jax.ShapeDtypeStruct((members, comp // LANES, LANES), F32)

    plain = jax.ShapeDtypeStruct((rows_dev, width), BF16)
    weight = jax.ShapeDtypeStruct((comp, width), BF16)
    ordered = call(
        functools.partial(order_kernel, groups), plain, 0, 2 * rows_dev * big, 4 * big, remote=2,
        scratch=[
            pltpu.VMEM(dest.shape, jnp.int32),
            pltpu.VMEM(embed.shape, BF16),
            pltpu.VMEM(embed.shape, BF16),
            pltpu.SemaphoreType.DMA((1 + rows_dev // ROW_STEP,)),
            pltpu.SemaphoreType.DMA((rows_dev // ROW_STEP,)),
        ],
        out_space=pltpu.HBM,
    )(*(in_hbm(a) for a in (dest, embed)))
    quad, linear, offset = call(
        weight_kernel, (weight, weight, jax.ShapeDtypeStruct((1, comp), F32)),
        0, 8 * comp * width, 8 * comp * width, remote=2,
        scratch=[
            pltpu.VMEM(variances.shape, BF16),
            pltpu.VMEM(means.shape, BF16),
            pltpu.SemaphoreType.DMA((2,)),
        ],
    )(*(in_hbm(a) for a in (variances, means)))
    mine = lax.all_to_all(
        ordered.reshape(groups, block, width), "narrow", split_axis=0, concat_axis=0, tiled=True
    ).reshape(rows_dev, width)
    resp, high, low, sent = call(
        functools.partial(score_kernel, scale), (resp_shape, plain, plain, sent_shape),
        4, 4 * big * comp, 6 * big + 4 * area,
    )(mine, quad, linear, offset)
    got = everyone(sent)
    for step in range(SINK - 1):
        resp, sent = call(
            functools.partial(balance_kernel, target), (resp_shape, sent_shape),
            2, 4 * area, 8 * area,
        )(got, resp)
        got = everyone(sent)
    sums = call(
        functools.partial(moment_kernel, target),
        jax.ShapeDtypeStruct((comp, 2 * width + LANES), F32), 5, 10 * big * comp,
        6 * big + 8 * area, scratch=[pltpu.VMEM((rows_dev, 2 * comp), BF16)],
    )(got, resp, mine, high, low)
    sent = sums.astype(jnp.float16).reshape(4, quarter, sums.shape[1])
    got = everyone(sent, axis_index_groups=blocks)
    sent = (SAFE * jnp.sum(got.astype(F32), axis=0)).astype(jnp.float16)
    got = everyone(sent.reshape(deep, quarter // deep, sent.shape[1]), axis_index_groups=lines)
    got = jnp.sum(got.astype(F32), axis=0)
    first, second = got[:, :width], got[:, width : 2 * width]
    units = (8.0, 2.0**-6, 2.0**-15, 2.0**-15)
    total = sum(u * got[:, 2 * width + 32 * i :][:, :1] for i, u in enumerate(units))
    new_mean = first / total
    new_var = second / total - new_mean * new_mean + 0.01
    done = jnp.concatenate([new_mean, new_var], axis=1).astype(jnp.float16)
    got = everyone(jnp.broadcast_to(done[None], (deep,) + done.shape), axis_index_groups=lines)
    here = got.reshape(1, quarter, 2 * width)
    got = everyone(jnp.broadcast_to(here, (4,) + here.shape[1:]), axis_index_groups=blocks)
    out = lax.optimization_barrier(got.reshape(comp, 2 * width))
    return (out[:, :width].astype(F32), out[:, width:].astype(F32))


def solution(mesh):
    return jax.shard_map(
        on_device,
        mesh=mesh,
        in_specs=(
            P(("wide", "narrow"), None),
            P(("wide", "narrow")),
            P("narrow", None),
            P("narrow", None),
        ),
        out_specs=(P("narrow", None), P("narrow", None)),
        check_vma=False,
    )
```

```python
import functools

import jax
import jax.numpy as jnp
from jax import lax
from jax.experimental import pallas as pl
from jax.experimental.pallas import tpu as pltpu
from jax.sharding import PartitionSpec as P

SINK = 3
LANES = 128
ROW_STEP = 256
SAFE = 0.25
F32 = jnp.float32
BF16 = jnp.bfloat16
VMEM_LIMIT = 24 * 1024 * 1024


def call(kernel, out_shape, n_in, flops, moved, remote=0, scratch=()):
    vmem = pl.BlockSpec(memory_space=pltpu.VMEM)
    hbm = pl.BlockSpec(memory_space=pltpu.HBM)
    return pl.pallas_call(
        kernel,
        out_shape=out_shape,
        in_specs=[vmem] * n_in + [hbm] * remote,
        out_specs=jax.tree.map(lambda _: vmem, out_shape),
        scratch_shapes=scratch,
        compiler_params=pltpu.CompilerParams(vmem_limit_bytes=VMEM_LIMIT),
        cost_estimate=pl.CostEstimate(flops=flops, bytes_accessed=moved, transcendentals=0),
    )


def dot_nt(a, b):
    return lax.dot_general(a, b, (((1,), (1,)), ((), ())), preferred_element_type=F32)


def dot_tn(a, b):
    return lax.dot_general(a, b, (((0,), (0,)), ((), ())), preferred_element_type=F32)


def prepare_kernel(
    groups, dest_hbm, var_hbm, mean_hbm, embed_hbm, out_ref, quad_ref, lin_ref, off_ref,
    dest_ref, var_ref, mean_ref, embed_ref, arrivals,
):
    rows, width = embed_ref.shape
    comp = mean_ref.shape[0]
    block = rows // groups
    spans = [slice(start, start + ROW_STEP) for start in range(0, rows, ROW_STEP)]
    pairs = [(dest_hbm, dest_ref), (var_hbm, var_ref), (mean_hbm, mean_ref)]
    pairs += [(embed_hbm.at[span], embed_ref.at[span]) for span in spans]
    loads = [pltpu.make_async_copy(*pair, arrivals.at[i]) for i, pair in enumerate(pairs)]
    for load in loads:
        load.start()
    loads[0].wait()
    before = lax.broadcasted_iota(jnp.int32, (LANES, LANES), 0)
    after = lax.broadcasted_iota(jnp.int32, (LANES, LANES), 1)
    earlier = jnp.where(before < after, 1.0, 0.0).astype(BF16)
    group = lax.broadcasted_iota(jnp.int32, (groups, LANES), 0)
    base = (group * block).astype(F32)
    count = jnp.zeros((groups, 1), F32)
    places = []
    for start in range(0, rows, LANES):
        hot = jnp.where(group == dest_ref[start : start + LANES][None, :], 1.0, 0.0)
        rank = jnp.dot(hot.astype(BF16), earlier, preferred_element_type=F32) + count
        places.append(jnp.sum(hot * (rank + base), axis=0, keepdims=True))
        count = count + jnp.sum(hot, axis=1, keepdims=True)
    place = jnp.concatenate(places, axis=1).astype(jnp.int32)
    loads[1].wait()
    loads[2].wait()
    offsets = []
    for start in range(0, comp, LANES):
        span = slice(start, start + LANES)
        var = var_ref[span, :].astype(F32)
        mean = mean_ref[span, :].astype(F32)
        prec = 1.0 / var
        scaled = mean * prec
        quad_ref[span, :] = (-0.5 * prec).astype(BF16)
        lin_ref[span, :] = scaled.astype(BF16)
        term = jnp.log(var) + mean * scaled
        part = sum(term[:, i : i + LANES] for i in range(0, width, LANES))
        offsets.append(-0.5 * jnp.sum(jnp.transpose(part), axis=0, keepdims=True))
    off_ref[...] = jnp.concatenate(offsets, axis=1)
    for load in loads[3:]:
        load.wait()
    for span in spans:
        slot = lax.broadcasted_iota(jnp.int32, (ROW_STEP, rows), 0) + span.start
        pick = jnp.where(slot == place, 1.0, 0.0).astype(BF16)
        got = jnp.dot(pick, embed_ref[...], preferred_element_type=F32)
        out_ref[span, :] = got.astype(BF16)


def put_mass(mass, sent_ref):
    for i in range(sent_ref.shape[1]):
        part = mass[:, i * LANES : (i + 1) * LANES]
        sent_ref[:, i, :] = jnp.broadcast_to(part, (sent_ref.shape[0], LANES))


def get_mass(got_ref):
    block = jnp.sum(got_ref[...], axis=0)
    return jnp.concatenate([block[i : i + 1] for i in range(block.shape[0])], axis=1)


def score_kernel(
    scale, x_ref, quad_ref, lin_ref, off_ref, resp_ref, high_ref, low_ref, sent_ref
):
    rows = x_ref.shape[0]
    mass = jnp.zeros((1, resp_ref.shape[1]), F32)
    for start in range(0, rows, ROW_STEP):
        span = slice(start, start + ROW_STEP)
        x = x_ref[span, :]
        wide = x.astype(F32)
        square = wide * wide
        high = square.astype(BF16)
        high_ref[span, :] = high
        low_ref[span, :] = (square - high.astype(F32)).astype(BF16)
        raw = dot_nt(high, quad_ref[...]) + dot_nt(x, lin_ref[...])
        score = scale * (raw + off_ref[...])
        lifted = jnp.exp(score - jnp.max(score, axis=1, keepdims=True))
        resp = lifted / jnp.sum(lifted, axis=1, keepdims=True)
        resp_ref[span, :] = resp
        mass = mass + jnp.sum(resp, axis=0, keepdims=True)
    put_mass(mass, sent_ref)


def balance_step(resp, pull):
    scaled = resp * pull
    return scaled / jnp.sum(scaled, axis=1, keepdims=True)


def balance_kernel(target, got_ref, resp_ref, out_ref, sent_ref):
    rows, comp = resp_ref.shape
    pull = target / get_mass(got_ref)
    mass = jnp.zeros((1, comp), F32)
    for start in range(0, rows, ROW_STEP):
        span = slice(start, start + ROW_STEP)
        resp = balance_step(resp_ref[span, :], pull)
        out_ref[span, :] = resp
        mass = mass + jnp.sum(resp, axis=0, keepdims=True)
    put_mass(mass, sent_ref)


def total_parts(total):
    coarse = jnp.floor(total / 8)
    rest = total - 8 * coarse
    middle = jnp.floor(rest * 2**6)
    rest = (rest - middle / 2**6) * 2**15
    fine = jnp.floor(rest)
    lane = lax.broadcasted_iota(jnp.int32, total.shape, 1)
    return jnp.where(
        lane < 64,
        jnp.where(lane < 32, coarse, middle),
        jnp.where(lane < 96, fine, rest - fine),
    )


def put_moments(both, x_ref, high_ref, low_ref, out_ref):
    part = out_ref.shape[0]
    width = x_ref.shape[1]
    first = dot_tn(both, x_ref[...])
    out_ref[:, :width] = first[:part] + first[part:]
    second = dot_tn(both, high_ref[...])
    out_ref[:, width : 2 * width] = (
        second[:part] + second[part:] + dot_tn(both[:, :part], low_ref[...])
    )
    total = dot_tn(both, jnp.ones((both.shape[0], LANES), BF16))
    out_ref[:, 2 * width :] = total_parts(total[:part] + total[part:])


def moment_kernel(
    target, got_ref, resp_ref, x_ref, high_ref, low_ref, out_ref, both_ref
):
    rows, comp = resp_ref.shape
    pull = target / get_mass(got_ref)
    for start in range(0, rows, ROW_STEP):
        span = slice(start, start + ROW_STEP)
        resp = balance_step(resp_ref[span, :], pull)
        high = resp.astype(BF16)
        both_ref[span, :comp] = high
        both_ref[span, comp:] = (resp - high.astype(F32)).astype(BF16)
    put_moments(both_ref[...], x_ref, high_ref, low_ref, out_ref)


def on_device(embed, dest, means, variances):
    rows_dev, width = embed.shape
    groups = lax.axis_size("narrow")
    members = lax.axis_size("wide")
    block = rows_dev // groups
    comp = means.shape[0]
    quarter = comp // 4
    deep = members // 4
    lines = [[4 * z + i for z in range(deep)] for i in range(4)]
    blocks = [[4 * z + i for i in range(4)] for z in range(deep)]
    scale = width ** (-0.5)
    target = float(rows_dev * members / comp)
    big = rows_dev * width
    area = rows_dev * comp

    everyone = functools.partial(
        lax.all_to_all, axis_name="wide", split_axis=0, concat_axis=0, tiled=True
    )
    resp_shape = jax.ShapeDtypeStruct((rows_dev, comp), F32)
    sent_shape = jax.ShapeDtypeStruct((members, comp // LANES, LANES), F32)

    plain = jax.ShapeDtypeStruct((rows_dev, width), BF16)
    weight = jax.ShapeDtypeStruct((comp, width), BF16)
    ordered, quad, linear, offset = call(
        functools.partial(prepare_kernel, groups),
        (plain, weight, weight, jax.ShapeDtypeStruct((1, comp), F32)),
        0, 2 * rows_dev * big, 4 * big, remote=4,
        scratch=[
            pltpu.VMEM(dest.shape, jnp.int32),
            pltpu.VMEM(variances.shape, BF16),
            pltpu.VMEM(means.shape, BF16),
            pltpu.VMEM(embed.shape, BF16),
            pltpu.SemaphoreType.DMA((3 + rows_dev // ROW_STEP,)),
        ],
    )(*(pltpu.with_memory_space_constraint(a, pltpu.HBM) for a in (dest, variances, means, embed)))
    mine = lax.all_to_all(
        ordered.reshape(groups, block, width), "narrow", split_axis=0, concat_axis=0, tiled=True
    ).reshape(rows_dev, width)
    resp, high, low, sent = call(
        functools.partial(score_kernel, scale), (resp_shape, plain, plain, sent_shape),
        4, 4 * big * comp, 6 * big + 4 * area,
    )(mine, quad, linear, offset)
    got = everyone(sent)
    for step in range(SINK - 1):
        resp, sent = call(
            functools.partial(balance_kernel, target), (resp_shape, sent_shape),
            2, 4 * area, 8 * area,
        )(got, resp)
        got = everyone(sent)
    sums = call(
        functools.partial(moment_kernel, target),
        jax.ShapeDtypeStruct((comp, 2 * width + LANES), F32), 5, 10 * big * comp,
        6 * big + 8 * area, scratch=[pltpu.VMEM((rows_dev, 2 * comp), BF16)],
    )(got, resp, mine, high, low)
    sent = sums.astype(jnp.float16).reshape(4, quarter, sums.shape[1])
    got = everyone(sent, axis_index_groups=blocks)
    sent = (SAFE * jnp.sum(got.astype(F32), axis=0)).astype(jnp.float16)
    got = everyone(sent.reshape(deep, quarter // deep, sent.shape[1]), axis_index_groups=lines)
    got = jnp.sum(got.astype(F32), axis=0)
    first, second = got[:, :width], got[:, width : 2 * width]
    units = (8.0, 2.0**-6, 2.0**-15, 2.0**-15)
    total = sum(u * got[:, 2 * width + 32 * i :][:, :1] for i, u in enumerate(units))
    new_mean = first / total
    new_var = second / total - new_mean * new_mean + 0.01
    done = jnp.concatenate([new_mean, new_var], axis=1).astype(jnp.float16)
    got = everyone(jnp.broadcast_to(done[None], (deep,) + done.shape), axis_index_groups=lines)
    here = got.reshape(1, quarter, 2 * width)
    got = everyone(jnp.broadcast_to(here, (4,) + here.shape[1:]), axis_index_groups=blocks)
    out = lax.optimization_barrier(got.reshape(comp, 2 * width))
    return (out[:, :width].astype(F32), out[:, width:].astype(F32))


def solution(mesh):
    return jax.shard_map(
        on_device,
        mesh=mesh,
        in_specs=(
            P(("wide", "narrow"), None),
            P(("wide", "narrow")),
            P("narrow", None),
            P("narrow", None),
        ),
        out_specs=(P("narrow", None), P("narrow", None)),
        check_vma=False,
    )
```

```python
import functools

import jax
import jax.numpy as jnp
from jax import lax
from jax.experimental import pallas as pl
from jax.experimental.pallas import tpu as pltpu
from jax.sharding import PartitionSpec as P

SINK = 3
LANES = 128
ROW_STEP = 256
SAFE = 0.25
F32 = jnp.float32
BF16 = jnp.bfloat16
VMEM_LIMIT = 24 * 1024 * 1024


def call(kernel, out_shape, n_in, flops, moved, remote=0, scratch=()):
    vmem = pl.BlockSpec(memory_space=pltpu.VMEM)
    hbm = pl.BlockSpec(memory_space=pltpu.HBM)
    return pl.pallas_call(
        kernel,
        out_shape=out_shape,
        in_specs=[vmem] * n_in + [hbm] * remote,
        out_specs=jax.tree.map(lambda _: vmem, out_shape),
        scratch_shapes=scratch,
        compiler_params=pltpu.CompilerParams(vmem_limit_bytes=VMEM_LIMIT),
        cost_estimate=pl.CostEstimate(flops=flops, bytes_accessed=moved, transcendentals=0),
    )


def dot_nt(a, b):
    return lax.dot_general(a, b, (((1,), (1,)), ((), ())), preferred_element_type=F32)


def dot_tn(a, b):
    return lax.dot_general(a, b, (((0,), (0,)), ((), ())), preferred_element_type=F32)


def prepare_kernel(
    groups, dest_hbm, var_hbm, mean_hbm, embed_hbm, out_ref, quad_ref, lin_ref, off_ref,
    dest_ref, var_ref, mean_ref, embed_ref, arrivals,
):
    rows, width = embed_ref.shape
    comp = mean_ref.shape[0]
    block = rows // groups
    spans = [slice(start, start + ROW_STEP) for start in range(0, rows, ROW_STEP)]
    pairs = [(dest_hbm, dest_ref), (var_hbm, var_ref), (mean_hbm, mean_ref)]
    pairs += [(embed_hbm.at[span], embed_ref.at[span]) for span in spans]
    loads = [pltpu.make_async_copy(*pair, arrivals.at[i]) for i, pair in enumerate(pairs)]
    for load in loads:
        load.start()
    loads[0].wait()
    before = lax.broadcasted_iota(jnp.int32, (LANES, LANES), 0)
    after = lax.broadcasted_iota(jnp.int32, (LANES, LANES), 1)
    earlier = jnp.where(before < after, 1.0, 0.0).astype(BF16)
    group = lax.broadcasted_iota(jnp.int32, (groups, LANES), 0)
    base = (group * block).astype(F32)
    count = jnp.zeros((groups, 1), F32)
    places = []
    for start in range(0, rows, LANES):
        hot = jnp.where(group == dest_ref[start : start + LANES][None, :], 1.0, 0.0)
        rank = jnp.dot(hot.astype(BF16), earlier, preferred_element_type=F32) + count
        places.append(jnp.sum(hot * (rank + base), axis=0, keepdims=True))
        count = count + jnp.sum(hot, axis=1, keepdims=True)
    place = jnp.concatenate(places, axis=1).astype(jnp.int32)
    loads[1].wait()
    loads[2].wait()
    offsets = []
    for start in range(0, comp, LANES):
        span = slice(start, start + LANES)
        var = var_ref[span, :].astype(F32)
        mean = mean_ref[span, :].astype(F32)
        prec = 1.0 / var
        scaled = mean * prec
        quad_ref[span, :] = (-0.5 * prec).astype(BF16)
        lin_ref[span, :] = scaled.astype(BF16)
        term = jnp.log(var) + mean * scaled
        part = sum(term[:, i : i + LANES] for i in range(0, width, LANES))
        offsets.append(-0.5 * jnp.sum(jnp.transpose(part), axis=0, keepdims=True))
    off_ref[...] = jnp.concatenate(offsets, axis=1)
    for load in loads[3:]:
        load.wait()
    for span in spans:
        slot = lax.broadcasted_iota(jnp.int32, (ROW_STEP, rows), 0) + span.start
        pick = jnp.where(slot == place, 1.0, 0.0).astype(BF16)
        got = jnp.dot(pick, embed_ref[...], preferred_element_type=F32)
        out_ref[span, :] = got.astype(BF16)


def put_mass(mass, sent_ref):
    for i in range(sent_ref.shape[1]):
        part = mass[:, i * LANES : (i + 1) * LANES]
        sent_ref[:, i, :] = jnp.broadcast_to(part, (sent_ref.shape[0], LANES))


def get_mass(got_ref):
    block = jnp.sum(got_ref[...], axis=0)
    return jnp.concatenate([block[i : i + 1] for i in range(block.shape[0])], axis=1)


def score_kernel(
    scale, x_ref, quad_ref, lin_ref, off_ref, resp_ref, high_ref, low_ref, sent_ref
):
    rows = x_ref.shape[0]
    mass = jnp.zeros((1, resp_ref.shape[1]), F32)
    for start in range(0, rows, ROW_STEP):
        span = slice(start, start + ROW_STEP)
        x = x_ref[span, :]
        wide = x.astype(F32)
        square = wide * wide
        high = square.astype(BF16)
        high_ref[span, :] = high
        low_ref[span, :] = (square - high.astype(F32)).astype(BF16)
        raw = dot_nt(high, quad_ref[...]) + dot_nt(x, lin_ref[...])
        score = scale * (raw + off_ref[...])
        lifted = jnp.exp(score - jnp.max(score, axis=1, keepdims=True))
        resp = lifted / jnp.sum(lifted, axis=1, keepdims=True)
        resp_ref[span, :] = resp
        mass = mass + jnp.sum(resp, axis=0, keepdims=True)
    put_mass(mass, sent_ref)


def balance_step(resp, pull):
    scaled = resp * pull
    return scaled / jnp.sum(scaled, axis=1, keepdims=True)


def balance_kernel(target, got_ref, resp_ref, out_ref, sent_ref):
    rows, comp = resp_ref.shape
    pull = target / get_mass(got_ref)
    mass = jnp.zeros((1, comp), F32)
    for start in range(0, rows, ROW_STEP):
        span = slice(start, start + ROW_STEP)
        resp = balance_step(resp_ref[span, :], pull)
        out_ref[span, :] = resp
        mass = mass + jnp.sum(resp, axis=0, keepdims=True)
    put_mass(mass, sent_ref)


def total_parts(total):
    coarse = jnp.floor(total / 8)
    rest = total - 8 * coarse
    middle = jnp.floor(rest * 2**6)
    rest = (rest - middle / 2**6) * 2**15
    fine = jnp.floor(rest)
    lane = lax.broadcasted_iota(jnp.int32, total.shape, 1)
    return jnp.where(
        lane < 64,
        jnp.where(lane < 32, coarse, middle),
        jnp.where(lane < 96, fine, rest - fine),
    )


def moment_kernel(target, got_ref, resp_ref, x_ref, high_ref, low_ref, out_ref, both_ref):
    rows, comp = resp_ref.shape
    width = x_ref.shape[1]
    pull = target / get_mass(got_ref)
    total = jnp.zeros((1, comp), F32)
    for start in range(0, rows, ROW_STEP):
        span = slice(start, start + ROW_STEP)
        resp = balance_step(resp_ref[span, :], pull)
        high = resp.astype(BF16)
        both_ref[span, :comp] = high
        both_ref[span, comp:] = (resp - high.astype(F32)).astype(BF16)
        total = total + jnp.sum(resp, axis=0, keepdims=True)
    both = both_ref[...]
    first = dot_tn(both, x_ref[...])
    out_ref[:, :width] = first[:comp] + first[comp:]
    second = dot_tn(both, high_ref[...])
    out_ref[:, width : 2 * width] = (
        second[:comp] + second[comp:] + dot_tn(both[:, :comp], low_ref[...])
    )
    out_ref[:, 2 * width :] = total_parts(jnp.transpose(jnp.broadcast_to(total, (LANES, comp))))


def on_device(embed, dest, means, variances):
    rows_dev, width = embed.shape
    groups = lax.axis_size("narrow")
    members = lax.axis_size("wide")
    block = rows_dev // groups
    comp = means.shape[0]
    quarter = comp // 4
    deep = members // 4
    lines = [[4 * z + i for z in range(deep)] for i in range(4)]
    blocks = [[4 * z + i for i in range(4)] for z in range(deep)]
    scale = width ** (-0.5)
    target = float(rows_dev * members / comp)
    big = rows_dev * width
    area = rows_dev * comp

    everyone = functools.partial(
        lax.all_to_all, axis_name="wide", split_axis=0, concat_axis=0, tiled=True
    )
    resp_shape = jax.ShapeDtypeStruct((rows_dev, comp), F32)
    sent_shape = jax.ShapeDtypeStruct((members, comp // LANES, LANES), F32)

    plain = jax.ShapeDtypeStruct((rows_dev, width), BF16)
    weight = jax.ShapeDtypeStruct((comp, width), BF16)
    ordered, quad, linear, offset = call(
        functools.partial(prepare_kernel, groups),
        (plain, weight, weight, jax.ShapeDtypeStruct((1, comp), F32)),
        0, 2 * rows_dev * big, 4 * big, remote=4,
        scratch=[
            pltpu.VMEM(dest.shape, jnp.int32),
            pltpu.VMEM(variances.shape, BF16),
            pltpu.VMEM(means.shape, BF16),
            pltpu.VMEM(embed.shape, BF16),
            pltpu.SemaphoreType.DMA((3 + rows_dev // ROW_STEP,)),
        ],
    )(*(pltpu.with_memory_space_constraint(a, pltpu.HBM) for a in (dest, variances, means, embed)))
    mine = lax.all_to_all(
        ordered.reshape(groups, block, width), "narrow", split_axis=0, concat_axis=0, tiled=True
    ).reshape(rows_dev, width)
    resp, high, low, sent = call(
        functools.partial(score_kernel, scale), (resp_shape, plain, plain, sent_shape),
        4, 4 * big * comp, 6 * big + 4 * area,
    )(mine, quad, linear, offset)
    got = everyone(sent)
    for step in range(SINK - 1):
        resp, sent = call(
            functools.partial(balance_kernel, target), (resp_shape, sent_shape),
            2, 4 * area, 8 * area,
        )(got, resp)
        got = everyone(sent)
    sums = call(
        functools.partial(moment_kernel, target),
        jax.ShapeDtypeStruct((comp, 2 * width + LANES), F32), 5, 10 * big * comp,
        6 * big + 8 * area, scratch=[pltpu.VMEM((rows_dev, 2 * comp), BF16)],
    )(got, resp, mine, high, low)
    sent = sums.astype(jnp.float16).reshape(4, quarter, sums.shape[1])
    got = everyone(sent, axis_index_groups=blocks)
    sent = (SAFE * jnp.sum(got.astype(F32), axis=0)).astype(jnp.float16)
    got = everyone(sent.reshape(deep, quarter // deep, sent.shape[1]), axis_index_groups=lines)
    got = jnp.sum(got.astype(F32), axis=0)
    first, second = got[:, :width], got[:, width : 2 * width]
    units = (8.0, 2.0**-6, 2.0**-15, 2.0**-15)
    total = sum(u * got[:, 2 * width + 32 * i :][:, :1] for i, u in enumerate(units))
    new_mean = first / total
    new_var = second / total - new_mean * new_mean + 0.01
    done = jnp.concatenate([new_mean, new_var], axis=1).astype(jnp.float16)
    got = everyone(jnp.broadcast_to(done[None], (deep,) + done.shape), axis_index_groups=lines)
    here = got.reshape(1, quarter, 2 * width)
    got = everyone(jnp.broadcast_to(here, (4,) + here.shape[1:]), axis_index_groups=blocks)
    out = lax.optimization_barrier(got.reshape(comp, 2 * width))
    return (out[:, :width].astype(F32), out[:, width:].astype(F32))


def solution(mesh):
    return jax.shard_map(
        on_device,
        mesh=mesh,
        in_specs=(
            P(("wide", "narrow"), None),
            P(("wide", "narrow")),
            P("narrow", None),
            P("narrow", None),
        ),
        out_specs=(P("narrow", None), P("narrow", None)),
        check_vma=False,
    )
```

```python
import functools

import jax
import jax.numpy as jnp
from jax import lax
from jax.experimental import pallas as pl
from jax.experimental.pallas import tpu as pltpu
from jax.sharding import PartitionSpec as P

SINK = 3
LANES = 128
ROW_STEP = 256
SAFE = 0.25
F32 = jnp.float32
BF16 = jnp.bfloat16
VMEM_LIMIT = 24 * 1024 * 1024


def call(kernel, out_shape, n_in, flops, moved, remote=0, scratch=()):
    vmem = pl.BlockSpec(memory_space=pltpu.VMEM)
    hbm = pl.BlockSpec(memory_space=pltpu.HBM)
    return pl.pallas_call(
        kernel,
        out_shape=out_shape,
        in_specs=[vmem] * n_in + [hbm] * remote,
        out_specs=jax.tree.map(lambda _: vmem, out_shape),
        scratch_shapes=scratch,
        compiler_params=pltpu.CompilerParams(vmem_limit_bytes=VMEM_LIMIT),
        cost_estimate=pl.CostEstimate(flops=flops, bytes_accessed=moved, transcendentals=0),
    )


def dot_nt(a, b):
    return lax.dot_general(a, b, (((1,), (1,)), ((), ())), preferred_element_type=F32)


def dot_tn(a, b):
    return lax.dot_general(a, b, (((0,), (0,)), ((), ())), preferred_element_type=F32)


def prepare_kernel(
    groups, dest_hbm, var_hbm, mean_hbm, embed_hbm, out_ref, quad_ref, lin_ref, off_ref,
    dest_ref, var_ref, mean_ref, embed_ref, arrivals,
):
    rows, width = embed_ref.shape
    comp = mean_ref.shape[0]
    block = rows // groups
    spans = [slice(start, start + ROW_STEP) for start in range(0, rows, ROW_STEP)]
    pairs = [(dest_hbm, dest_ref), (var_hbm, var_ref), (mean_hbm, mean_ref)]
    pairs += [(embed_hbm.at[span], embed_ref.at[span]) for span in spans]
    loads = [pltpu.make_async_copy(*pair, arrivals.at[i]) for i, pair in enumerate(pairs)]
    for load in loads:
        load.start()
    loads[0].wait()
    before = lax.broadcasted_iota(jnp.int32, (LANES, LANES), 0)
    after = lax.broadcasted_iota(jnp.int32, (LANES, LANES), 1)
    earlier = jnp.where(before < after, 1.0, 0.0).astype(BF16)
    group = lax.broadcasted_iota(jnp.int32, (groups, LANES), 0)
    base = (group * block).astype(F32)
    count = jnp.zeros((groups, 1), F32)
    places = []
    for start in range(0, rows, LANES):
        hot = jnp.where(group == dest_ref[start : start + LANES][None, :], 1.0, 0.0)
        rank = jnp.dot(hot.astype(BF16), earlier, preferred_element_type=F32) + count
        places.append(jnp.sum(hot * (rank + base), axis=0, keepdims=True))
        count = count + jnp.sum(hot, axis=1, keepdims=True)
    place = jnp.concatenate(places, axis=1).astype(jnp.int32)
    loads[1].wait()
    loads[2].wait()
    offsets = []
    for start in range(0, comp, LANES):
        span = slice(start, start + LANES)
        var = var_ref[span, :].astype(F32)
        mean = mean_ref[span, :].astype(F32)
        prec = 1.0 / var
        scaled = mean * prec
        quad_ref[span, :] = (-0.5 * prec).astype(BF16)
        lin_ref[span, :] = scaled.astype(BF16)
        term = jnp.log(var) + mean * scaled
        part = sum(term[:, i : i + LANES] for i in range(0, width, LANES))
        offsets.append(-0.5 * jnp.sum(jnp.transpose(part), axis=0, keepdims=True))
    off_ref[...] = jnp.concatenate(offsets, axis=1)
    for load in loads[3:]:
        load.wait()
    for span in spans:
        slot = lax.broadcasted_iota(jnp.int32, (ROW_STEP, rows), 0) + span.start
        pick = jnp.where(slot == place, 1.0, 0.0).astype(BF16)
        got = jnp.dot(pick, embed_ref[...], preferred_element_type=F32)
        out_ref[span, :] = got.astype(BF16)


def put_mass(mass, sent_ref):
    for i in range(sent_ref.shape[1]):
        part = mass[:, i * LANES : (i + 1) * LANES]
        sent_ref[:, i, :] = jnp.broadcast_to(part, (sent_ref.shape[0], LANES))


def get_mass(got_ref):
    block = jnp.sum(got_ref[...], axis=0)
    return jnp.concatenate([block[i : i + 1] for i in range(block.shape[0])], axis=1)


def score_kernel(
    scale, x_ref, quad_ref, lin_ref, off_ref, resp_ref, high_ref, low_ref, sent_ref
):
    rows = x_ref.shape[0]
    mass = jnp.zeros((1, resp_ref.shape[1]), F32)
    for start in range(0, rows, ROW_STEP):
        span = slice(start, start + ROW_STEP)
        x = x_ref[span, :]
        wide = x.astype(F32)
        square = wide * wide
        high = square.astype(BF16)
        high_ref[span, :] = high
        low_ref[span, :] = (square - high.astype(F32)).astype(BF16)
        raw = dot_nt(high, quad_ref[...]) + dot_nt(x, lin_ref[...])
        score = scale * (raw + off_ref[...])
        lifted = jnp.exp(score - jnp.max(score, axis=1, keepdims=True))
        resp = lifted / jnp.sum(lifted, axis=1, keepdims=True)
        resp_ref[span, :] = resp
        mass = mass + jnp.sum(resp, axis=0, keepdims=True)
    put_mass(mass, sent_ref)


def balance_step(resp, pull):
    scaled = resp * pull
    return scaled / jnp.sum(scaled, axis=1, keepdims=True)


def balance_kernel(target, got_ref, resp_ref, out_ref, sent_ref):
    rows, comp = resp_ref.shape
    pull = target / get_mass(got_ref)
    mass = jnp.zeros((1, comp), F32)
    for start in range(0, rows, ROW_STEP):
        span = slice(start, start + ROW_STEP)
        resp = balance_step(resp_ref[span, :], pull)
        out_ref[span, :] = resp
        mass = mass + jnp.sum(resp, axis=0, keepdims=True)
    put_mass(mass, sent_ref)


def total_parts(total):
    coarse = jnp.floor(total / 8)
    rest = total - 8 * coarse
    middle = jnp.floor(rest * 2**6)
    rest = (rest - middle / 2**6) * 2**15
    fine = jnp.floor(rest)
    lane = lax.broadcasted_iota(jnp.int32, total.shape, 1)
    return jnp.where(
        lane < 64,
        jnp.where(lane < 32, coarse, middle),
        jnp.where(lane < 96, fine, rest - fine),
    )


def moment_kernel(target, got_ref, resp_ref, x_ref, high_ref, low_ref, out_ref, both_ref):
    rows, comp = resp_ref.shape
    width = x_ref.shape[1]
    pull = target / get_mass(got_ref)
    total = jnp.zeros((1, comp), F32)
    for start in range(0, rows, ROW_STEP):
        span = slice(start, start + ROW_STEP)
        resp = balance_step(resp_ref[span, :], pull)
        high = resp.astype(BF16)
        both_ref[span, :comp] = high
        both_ref[span, comp:] = (resp - high.astype(F32)).astype(BF16)
        total = total + jnp.sum(resp, axis=0, keepdims=True)
    both = both_ref[...]
    first = dot_tn(both, x_ref[...])
    out_ref[:, :width] = first[:comp] + first[comp:]
    second = dot_tn(both, high_ref[...])
    out_ref[:, width : 2 * width] = (
        second[:comp] + second[comp:] + dot_tn(both[:, :comp], low_ref[...])
    )
    out_ref[:, 2 * width :] = total_parts(jnp.transpose(jnp.broadcast_to(total, (LANES, comp))))


def on_device(embed, dest, means, variances):
    rows_dev, width = embed.shape
    groups = lax.axis_size("narrow")
    members = lax.axis_size("wide")
    block = rows_dev // groups
    comp = means.shape[0]
    quarter = comp // 4
    deep = members // 4
    lines = [[4 * z + i for z in range(deep)] for i in range(4)]
    blocks = [[4 * z + i for i in range(4)] for z in range(deep)]
    scale = width ** (-0.5)
    target = float(rows_dev * members / comp)
    big = rows_dev * width
    area = rows_dev * comp

    everyone = functools.partial(
        lax.all_to_all, axis_name="wide", split_axis=0, concat_axis=0, tiled=True
    )
    resp_shape = jax.ShapeDtypeStruct((rows_dev, comp), F32)
    sent_shape = jax.ShapeDtypeStruct((members, comp // LANES, LANES), F32)

    plain = jax.ShapeDtypeStruct((rows_dev, width), BF16)
    weight = jax.ShapeDtypeStruct((comp, width), BF16)
    ordered, quad, linear, offset = call(
        functools.partial(prepare_kernel, groups),
        (plain, weight, weight, jax.ShapeDtypeStruct((1, comp), F32)),
        0, 2 * rows_dev * big, 4 * big, remote=4,
        scratch=[
            pltpu.VMEM(dest.shape, jnp.int32),
            pltpu.VMEM(variances.shape, BF16),
            pltpu.VMEM(means.shape, BF16),
            pltpu.VMEM(embed.shape, BF16),
            pltpu.SemaphoreType.DMA((3 + rows_dev // ROW_STEP,)),
        ],
    )(*(pltpu.with_memory_space_constraint(a, pltpu.HBM) for a in (dest, variances, means, embed)))
    mine = lax.all_to_all(
        ordered.reshape(groups, block, width), "narrow", split_axis=0, concat_axis=0, tiled=True
    ).reshape(rows_dev, width)
    resp, high, low, sent = call(
        functools.partial(score_kernel, scale), (resp_shape, plain, plain, sent_shape),
        4, 4 * big * comp, 6 * big + 4 * area,
    )(mine, quad, linear, offset)
    got = everyone(sent)
    for step in range(SINK - 1):
        resp, sent = call(
            functools.partial(balance_kernel, target), (resp_shape, sent_shape),
            2, 4 * area, 8 * area,
        )(got, resp)
        got = everyone(sent)
    sums = call(
        functools.partial(moment_kernel, target),
        jax.ShapeDtypeStruct((comp, 2 * width + LANES), F32), 5, 10 * big * comp,
        6 * big + 8 * area, scratch=[pltpu.VMEM((rows_dev, 2 * comp), BF16)],
    )(got, resp, mine, high, low)
    sent = sums.astype(jnp.float16).reshape(4, quarter, sums.shape[1])
    got = everyone(sent, axis_index_groups=blocks)
    sent = (SAFE * sum(got[i].astype(F32) for i in range(4))).astype(jnp.float16)
    got = everyone(sent.reshape(deep, quarter // deep, sent.shape[1]), axis_index_groups=lines)
    got = sum(got[i].astype(F32) for i in range(deep))
    first, second = got[:, :width], got[:, width : 2 * width]
    units = (8.0, 2.0**-6, 2.0**-15, 2.0**-15)
    total = sum(u * got[:, 2 * width + 32 * i :][:, :1] for i, u in enumerate(units))
    new_mean = first / total
    new_var = second / total - new_mean * new_mean + 0.01
    done = jnp.concatenate([new_mean, new_var], axis=1).astype(jnp.float16)
    got = everyone(jnp.broadcast_to(done[None], (deep,) + done.shape), axis_index_groups=lines)
    here = got.reshape(1, quarter, 2 * width)
    got = everyone(jnp.broadcast_to(here, (4,) + here.shape[1:]), axis_index_groups=blocks)
    out = lax.optimization_barrier(got.reshape(comp, 2 * width))
    return (out[:, :width].astype(F32), out[:, width:].astype(F32))


def solution(mesh):
    return jax.shard_map(
        on_device,
        mesh=mesh,
        in_specs=(
            P(("wide", "narrow"), None),
            P(("wide", "narrow")),
            P("narrow", None),
            P("narrow", None),
        ),
        out_specs=(P("narrow", None), P("narrow", None)),
        check_vma=False,
    )
```

```python
import functools

import jax
import jax.numpy as jnp
from jax import lax
from jax.experimental import pallas as pl
from jax.experimental.pallas import tpu as pltpu
from jax.sharding import PartitionSpec as P

SINK = 3
LANES = 128
ROW_STEP = 256
SAFE = 0.25
F32 = jnp.float32
BF16 = jnp.bfloat16
VMEM_LIMIT = 24 * 1024 * 1024


def call(kernel, out_shape, n_in, flops, moved, remote=0, scratch=()):
    vmem = pl.BlockSpec(memory_space=pltpu.VMEM)
    hbm = pl.BlockSpec(memory_space=pltpu.HBM)
    return pl.pallas_call(
        kernel,
        out_shape=out_shape,
        in_specs=[vmem] * n_in + [hbm] * remote,
        out_specs=jax.tree.map(lambda _: vmem, out_shape),
        scratch_shapes=scratch,
        compiler_params=pltpu.CompilerParams(vmem_limit_bytes=VMEM_LIMIT),
        cost_estimate=pl.CostEstimate(flops=flops, bytes_accessed=moved, transcendentals=0),
    )


def dot_nt(a, b):
    return lax.dot_general(a, b, (((1,), (1,)), ((), ())), preferred_element_type=F32)


def dot_tn(a, b):
    return lax.dot_general(a, b, (((0,), (0,)), ((), ())), preferred_element_type=F32)


def prepare_kernel(
    groups, dest_hbm, var_hbm, mean_hbm, embed_hbm, out_ref, quad_ref, lin_ref, off_ref,
    dest_ref, var_ref, mean_ref, embed_ref, arrivals,
):
    rows, width = embed_ref.shape
    comp = mean_ref.shape[0]
    block = rows // groups
    spans = [slice(start, start + ROW_STEP) for start in range(0, rows, ROW_STEP)]
    pairs = [(dest_hbm, dest_ref), (var_hbm, var_ref), (mean_hbm, mean_ref)]
    pairs += [(embed_hbm.at[span], embed_ref.at[span]) for span in spans]
    loads = [pltpu.make_async_copy(*pair, arrivals.at[i]) for i, pair in enumerate(pairs)]
    for load in loads:
        load.start()
    loads[0].wait()
    before = lax.broadcasted_iota(jnp.int32, (LANES, LANES), 0)
    after = lax.broadcasted_iota(jnp.int32, (LANES, LANES), 1)
    earlier = jnp.where(before < after, 1.0, 0.0).astype(BF16)
    group = lax.broadcasted_iota(jnp.int32, (groups, LANES), 0)
    base = (group * block).astype(F32)
    count = jnp.zeros((groups, 1), F32)
    places = []
    for start in range(0, rows, LANES):
        hot = jnp.where(group == dest_ref[start : start + LANES][None, :], 1.0, 0.0)
        rank = jnp.dot(hot.astype(BF16), earlier, preferred_element_type=F32) + count
        places.append(jnp.sum(hot * (rank + base), axis=0, keepdims=True))
        count = count + jnp.sum(hot, axis=1, keepdims=True)
    place = jnp.concatenate(places, axis=1).astype(jnp.int32)
    loads[1].wait()
    loads[2].wait()
    offsets = []
    for start in range(0, comp, LANES):
        span = slice(start, start + LANES)
        var = var_ref[span, :].astype(F32)
        mean = mean_ref[span, :].astype(F32)
        prec = 1.0 / var
        scaled = mean * prec
        quad_ref[span, :] = (-0.5 * prec).astype(BF16)
        lin_ref[span, :] = scaled.astype(BF16)
        term = jnp.log(var) + mean * scaled
        part = sum(term[:, i : i + LANES] for i in range(0, width, LANES))
        offsets.append(-0.5 * jnp.sum(jnp.transpose(part), axis=0, keepdims=True))
    off_ref[...] = jnp.concatenate(offsets, axis=1)
    for load in loads[3:]:
        load.wait()
    for span in spans:
        slot = lax.broadcasted_iota(jnp.int32, (ROW_STEP, rows), 0) + span.start
        pick = jnp.where(slot == place, 1.0, 0.0).astype(BF16)
        got = jnp.dot(pick, embed_ref[...], preferred_element_type=F32)
        out_ref[span, :] = got.astype(BF16)


def put_mass(mass, sent_ref):
    for i in range(sent_ref.shape[1]):
        part = mass[:, i * LANES : (i + 1) * LANES]
        sent_ref[:, i, :] = jnp.broadcast_to(part, (sent_ref.shape[0], LANES))


def get_mass(got_ref):
    block = jnp.sum(got_ref[...], axis=0)
    return jnp.concatenate([block[i : i + 1] for i in range(block.shape[0])], axis=1)


def score_kernel(
    scale, x_ref, quad_ref, lin_ref, off_ref, resp_ref, high_ref, low_ref, sent_ref
):
    rows = x_ref.shape[0]
    mass = jnp.zeros((1, resp_ref.shape[1]), F32)
    for start in range(0, rows, ROW_STEP):
        span = slice(start, start + ROW_STEP)
        x = x_ref[span, :]
        wide = x.astype(F32)
        square = wide * wide
        high = square.astype(BF16)
        high_ref[span, :] = high
        low_ref[span, :] = (square - high.astype(F32)).astype(BF16)
        raw = dot_nt(high, quad_ref[...]) + dot_nt(x, lin_ref[...])
        score = scale * (raw + off_ref[...])
        lifted = jnp.exp(score - jnp.max(score, axis=1, keepdims=True))
        resp = lifted / jnp.sum(lifted, axis=1, keepdims=True)
        resp_ref[span, :] = resp
        mass = mass + jnp.sum(resp, axis=0, keepdims=True)
    put_mass(mass, sent_ref)


def balance_step(resp, pull):
    scaled = resp * pull
    return scaled / jnp.sum(scaled, axis=1, keepdims=True)


def balance_kernel(target, got_ref, resp_ref, out_ref, sent_ref):
    rows, comp = resp_ref.shape
    pull = target / get_mass(got_ref)
    mass = jnp.zeros((1, comp), F32)
    for start in range(0, rows, ROW_STEP):
        span = slice(start, start + ROW_STEP)
        resp = balance_step(resp_ref[span, :], pull)
        out_ref[span, :] = resp
        mass = mass + jnp.sum(resp, axis=0, keepdims=True)
    put_mass(mass, sent_ref)


def total_parts(total):
    coarse = jnp.floor(total / 8)
    rest = total - 8 * coarse
    middle = jnp.floor(rest * 2**6)
    rest = (rest - middle / 2**6) * 2**15
    fine = jnp.floor(rest)
    lane = lax.broadcasted_iota(jnp.int32, total.shape, 1)
    return jnp.where(
        lane < 64,
        jnp.where(lane < 32, coarse, middle),
        jnp.where(lane < 96, fine, rest - fine),
    )


def put_moments(both, x_ref, high_ref, low_ref, out_ref):
    part = out_ref.shape[0]
    width = x_ref.shape[1]
    first = dot_tn(both, x_ref[...])
    out_ref[:, :width] = first[:part] + first[part:]
    second = dot_tn(both, high_ref[...])
    out_ref[:, width : 2 * width] = (
        second[:part] + second[part:] + dot_tn(both[:, :part], low_ref[...])
    )
    total = dot_tn(both, jnp.ones((both.shape[0], LANES), BF16))
    out_ref[:, 2 * width :] = total_parts(total[:part] + total[part:])


def moment_kernel(
    target, got_ref, resp_ref, x_ref, high_ref, low_ref, out_ref, both_ref
):
    rows, comp = resp_ref.shape
    pull = target / get_mass(got_ref)
    for start in range(0, rows, ROW_STEP):
        span = slice(start, start + ROW_STEP)
        resp = balance_step(resp_ref[span, :], pull)
        high = resp.astype(BF16)
        both_ref[span, :comp] = high
        both_ref[span, comp:] = (resp - high.astype(F32)).astype(BF16)
    put_moments(both_ref[...], x_ref, high_ref, low_ref, out_ref)


def on_device(embed, dest, means, variances):
    rows_dev, width = embed.shape
    groups = lax.axis_size("narrow")
    members = lax.axis_size("wide")
    block = rows_dev // groups
    comp = means.shape[0]
    quarter = comp // 4
    deep = members // 4
    lines = [[4 * z + i for z in range(deep)] for i in range(4)]
    blocks = [[4 * z + i for i in range(4)] for z in range(deep)]
    scale = width ** (-0.5)
    target = float(rows_dev * members / comp)
    big = rows_dev * width
    area = rows_dev * comp

    everyone = functools.partial(
        lax.all_to_all, axis_name="wide", split_axis=0, concat_axis=0, tiled=True
    )
    resp_shape = jax.ShapeDtypeStruct((rows_dev, comp), F32)
    sent_shape = jax.ShapeDtypeStruct((members, comp // LANES, LANES), F32)

    plain = jax.ShapeDtypeStruct((rows_dev, width), BF16)
    weight = jax.ShapeDtypeStruct((comp, width), BF16)
    ordered, quad, linear, offset = call(
        functools.partial(prepare_kernel, groups),
        (plain, weight, weight, jax.ShapeDtypeStruct((1, comp), F32)),
        0, 2 * rows_dev * big, 4 * big, remote=4,
        scratch=[
            pltpu.VMEM(dest.shape, jnp.int32),
            pltpu.VMEM(variances.shape, BF16),
            pltpu.VMEM(means.shape, BF16),
            pltpu.VMEM(embed.shape, BF16),
            pltpu.SemaphoreType.DMA((3 + rows_dev // ROW_STEP,)),
        ],
    )(*(pltpu.with_memory_space_constraint(a, pltpu.HBM) for a in (dest, variances, means, embed)))
    mine = lax.all_to_all(
        ordered.reshape(groups, block, width), "narrow", split_axis=0, concat_axis=0, tiled=True
    ).reshape(rows_dev, width)
    resp, high, low, sent = call(
        functools.partial(score_kernel, scale), (resp_shape, plain, plain, sent_shape),
        4, 4 * big * comp, 6 * big + 4 * area,
    )(mine, quad, linear, offset)
    got = everyone(sent)
    for step in range(SINK - 1):
        resp, sent = call(
            functools.partial(balance_kernel, target), (resp_shape, sent_shape),
            2, 4 * area, 8 * area,
        )(got, resp)
        got = everyone(sent)
    sums = call(
        functools.partial(moment_kernel, target),
        jax.ShapeDtypeStruct((comp, 2 * width + LANES), F32), 5, 10 * big * comp,
        6 * big + 8 * area, scratch=[pltpu.VMEM((rows_dev, 2 * comp), BF16)],
    )(got, resp, mine, high, low)
    sent = sums.astype(jnp.float16).reshape(4, quarter, sums.shape[1])
    got = everyone(sent, axis_index_groups=blocks)
    sent = (SAFE * sum(got[i].astype(F32) for i in range(4))).astype(jnp.float16)
    got = everyone(sent.reshape(deep, quarter // deep, sent.shape[1]), axis_index_groups=lines)
    got = sum(got[i].astype(F32) for i in range(deep))
    first, second = got[:, :width], got[:, width : 2 * width]
    units = (8.0, 2.0**-6, 2.0**-15, 2.0**-15)
    total = sum(u * got[:, 2 * width + 32 * i :][:, :1] for i, u in enumerate(units))
    new_mean = first / total
    new_var = second / total - new_mean * new_mean + 0.01
    done = jnp.concatenate([new_mean, new_var], axis=1).astype(jnp.float16)
    got = everyone(jnp.broadcast_to(done[None], (deep,) + done.shape), axis_index_groups=lines)
    here = got.reshape(1, quarter, 2 * width)
    got = everyone(jnp.broadcast_to(here, (4,) + here.shape[1:]), axis_index_groups=blocks)
    out = lax.optimization_barrier(got.reshape(comp, 2 * width))
    return (out[:, :width].astype(F32), out[:, width:].astype(F32))


def solution(mesh):
    return jax.shard_map(
        on_device,
        mesh=mesh,
        in_specs=(
            P(("wide", "narrow"), None),
            P(("wide", "narrow")),
            P("narrow", None),
            P("narrow", None),
        ),
        out_specs=(P("narrow", None), P("narrow", None)),
        check_vma=False,
    )
```

```python
import functools

import jax
import jax.numpy as jnp
from jax import lax
from jax.experimental import pallas as pl
from jax.experimental.pallas import tpu as pltpu
from jax.sharding import PartitionSpec as P

SINK = 3
LANES = 128
ROW_STEP = 384
SAFE = 0.25
F32 = jnp.float32
BF16 = jnp.bfloat16
VMEM_LIMIT = 24 * 1024 * 1024


def call(kernel, out_shape, n_in, flops, moved, remote=0, scratch=()):
    vmem = pl.BlockSpec(memory_space=pltpu.VMEM)
    hbm = pl.BlockSpec(memory_space=pltpu.HBM)
    return pl.pallas_call(
        kernel,
        out_shape=out_shape,
        in_specs=[vmem] * n_in + [hbm] * remote,
        out_specs=jax.tree.map(lambda _: vmem, out_shape),
        scratch_shapes=scratch,
        compiler_params=pltpu.CompilerParams(vmem_limit_bytes=VMEM_LIMIT),
        cost_estimate=pl.CostEstimate(flops=flops, bytes_accessed=moved, transcendentals=0),
    )


def dot_nt(a, b):
    return lax.dot_general(a, b, (((1,), (1,)), ((), ())), preferred_element_type=F32)


def dot_tn(a, b):
    return lax.dot_general(a, b, (((0,), (0,)), ((), ())), preferred_element_type=F32)


def prepare_kernel(
    groups, dest_hbm, var_hbm, mean_hbm, embed_hbm, out_ref, quad_ref, lin_ref, off_ref,
    dest_ref, var_ref, mean_ref, embed_ref, arrivals,
):
    rows, width = embed_ref.shape
    comp = mean_ref.shape[0]
    block = rows // groups
    spans = [slice(start, start + ROW_STEP) for start in range(0, rows, ROW_STEP)]
    pairs = [(dest_hbm, dest_ref), (var_hbm, var_ref), (mean_hbm, mean_ref)]
    pairs += [(embed_hbm.at[span], embed_ref.at[span]) for span in spans]
    loads = [pltpu.make_async_copy(*pair, arrivals.at[i]) for i, pair in enumerate(pairs)]
    for load in loads:
        load.start()
    loads[0].wait()
    before = lax.broadcasted_iota(jnp.int32, (LANES, LANES), 0)
    after = lax.broadcasted_iota(jnp.int32, (LANES, LANES), 1)
    earlier = jnp.where(before < after, 1.0, 0.0).astype(BF16)
    group = lax.broadcasted_iota(jnp.int32, (groups, LANES), 0)
    base = (group * block).astype(F32)
    count = jnp.zeros((groups, 1), F32)
    places = []
    for start in range(0, rows, LANES):
        hot = jnp.where(group == dest_ref[start : start + LANES][None, :], 1.0, 0.0)
        rank = jnp.dot(hot.astype(BF16), earlier, preferred_element_type=F32) + count
        places.append(jnp.sum(hot * (rank + base), axis=0, keepdims=True))
        count = count + jnp.sum(hot, axis=1, keepdims=True)
    place = jnp.concatenate(places, axis=1).astype(jnp.int32)
    loads[1].wait()
    loads[2].wait()
    offsets = []
    for start in range(0, comp, LANES):
        span = slice(start, start + LANES)
        var = var_ref[span, :].astype(F32)
        mean = mean_ref[span, :].astype(F32)
        prec = 1.0 / var
        scaled = mean * prec
        quad_ref[span, :] = (-0.5 * prec).astype(BF16)
        lin_ref[span, :] = scaled.astype(BF16)
        term = jnp.log(var) + mean * scaled
        part = sum(term[:, i : i + LANES] for i in range(0, width, LANES))
        offsets.append(-0.5 * jnp.sum(jnp.transpose(part), axis=0, keepdims=True))
    off_ref[...] = jnp.concatenate(offsets, axis=1)
    for load in loads[3:]:
        load.wait()
    for span in spans:
        slot = lax.broadcasted_iota(jnp.int32, (ROW_STEP, rows), 0) + span.start
        pick = jnp.where(slot == place, 1.0, 0.0).astype(BF16)
        got = jnp.dot(pick, embed_ref[...], preferred_element_type=F32)
        out_ref[span, :] = got.astype(BF16)


def put_mass(mass, sent_ref):
    for i in range(sent_ref.shape[1]):
        part = mass[:, i * LANES : (i + 1) * LANES]
        sent_ref[:, i, :] = jnp.broadcast_to(part, (sent_ref.shape[0], LANES))


def get_mass(got_ref):
    block = jnp.sum(got_ref[...], axis=0)
    return jnp.concatenate([block[i : i + 1] for i in range(block.shape[0])], axis=1)


def score_kernel(
    scale, x_ref, quad_ref, lin_ref, off_ref, resp_ref, high_ref, low_ref, sent_ref
):
    rows = x_ref.shape[0]
    mass = jnp.zeros((1, resp_ref.shape[1]), F32)
    for start in range(0, rows, ROW_STEP):
        span = slice(start, start + ROW_STEP)
        x = x_ref[span, :]
        wide = x.astype(F32)
        square = wide * wide
        high = square.astype(BF16)
        high_ref[span, :] = high
        low_ref[span, :] = (square - high.astype(F32)).astype(BF16)
        raw = dot_nt(high, quad_ref[...]) + dot_nt(x, lin_ref[...])
        score = scale * (raw + off_ref[...])
        lifted = jnp.exp(score - jnp.max(score, axis=1, keepdims=True))
        resp = lifted / jnp.sum(lifted, axis=1, keepdims=True)
        resp_ref[span, :] = resp
        mass = mass + jnp.sum(resp, axis=0, keepdims=True)
    put_mass(mass, sent_ref)


def balance_step(resp, pull):
    scaled = resp * pull
    return scaled / jnp.sum(scaled, axis=1, keepdims=True)


def balance_kernel(target, got_ref, resp_ref, out_ref, sent_ref):
    rows, comp = resp_ref.shape
    pull = target / get_mass(got_ref)
    mass = jnp.zeros((1, comp), F32)
    for start in range(0, rows, ROW_STEP):
        span = slice(start, start + ROW_STEP)
        resp = balance_step(resp_ref[span, :], pull)
        out_ref[span, :] = resp
        mass = mass + jnp.sum(resp, axis=0, keepdims=True)
    put_mass(mass, sent_ref)


def total_parts(total):
    coarse = jnp.floor(total / 8)
    rest = total - 8 * coarse
    middle = jnp.floor(rest * 2**6)
    rest = (rest - middle / 2**6) * 2**15
    fine = jnp.floor(rest)
    lane = lax.broadcasted_iota(jnp.int32, total.shape, 1)
    return jnp.where(
        lane < 64,
        jnp.where(lane < 32, coarse, middle),
        jnp.where(lane < 96, fine, rest - fine),
    )


def put_moments(both, x_ref, high_ref, low_ref, out_ref):
    part = out_ref.shape[0]
    width = x_ref.shape[1]
    first = dot_tn(both, x_ref[...])
    out_ref[:, :width] = first[:part] + first[part:]
    second = dot_tn(both, high_ref[...])
    out_ref[:, width : 2 * width] = (
        second[:part] + second[part:] + dot_tn(both[:, :part], low_ref[...])
    )
    total = dot_tn(both, jnp.ones((both.shape[0], LANES), BF16))
    out_ref[:, 2 * width :] = total_parts(total[:part] + total[part:])


def moment_kernel(
    target, got_ref, resp_ref, x_ref, high_ref, low_ref, out_ref, both_ref
):
    rows, comp = resp_ref.shape
    pull = target / get_mass(got_ref)
    for start in range(0, rows, ROW_STEP):
        span = slice(start, start + ROW_STEP)
        resp = balance_step(resp_ref[span, :], pull)
        high = resp.astype(BF16)
        both_ref[span, :comp] = high
        both_ref[span, comp:] = (resp - high.astype(F32)).astype(BF16)
    put_moments(both_ref[...], x_ref, high_ref, low_ref, out_ref)


def on_device(embed, dest, means, variances):
    rows_dev, width = embed.shape
    groups = lax.axis_size("narrow")
    members = lax.axis_size("wide")
    block = rows_dev // groups
    comp = means.shape[0]
    quarter = comp // 4
    deep = members // 4
    lines = [[4 * z + i for z in range(deep)] for i in range(4)]
    blocks = [[4 * z + i for i in range(4)] for z in range(deep)]
    scale = width ** (-0.5)
    target = float(rows_dev * members / comp)
    big = rows_dev * width
    area = rows_dev * comp

    everyone = functools.partial(
        lax.all_to_all, axis_name="wide", split_axis=0, concat_axis=0, tiled=True
    )
    resp_shape = jax.ShapeDtypeStruct((rows_dev, comp), F32)
    sent_shape = jax.ShapeDtypeStruct((members, comp // LANES, LANES), F32)

    plain = jax.ShapeDtypeStruct((rows_dev, width), BF16)
    weight = jax.ShapeDtypeStruct((comp, width), BF16)
    ordered, quad, linear, offset = call(
        functools.partial(prepare_kernel, groups),
        (plain, weight, weight, jax.ShapeDtypeStruct((1, comp), F32)),
        0, 2 * rows_dev * big, 4 * big, remote=4,
        scratch=[
            pltpu.VMEM(dest.shape, jnp.int32),
            pltpu.VMEM(variances.shape, BF16),
            pltpu.VMEM(means.shape, BF16),
            pltpu.VMEM(embed.shape, BF16),
            pltpu.SemaphoreType.DMA((3 + rows_dev // ROW_STEP,)),
        ],
    )(*(pltpu.with_memory_space_constraint(a, pltpu.HBM) for a in (dest, variances, means, embed)))
    mine = lax.all_to_all(
        ordered.reshape(groups, block, width), "narrow", split_axis=0, concat_axis=0, tiled=True
    ).reshape(rows_dev, width)
    resp, high, low, sent = call(
        functools.partial(score_kernel, scale), (resp_shape, plain, plain, sent_shape),
        4, 4 * big * comp, 6 * big + 4 * area,
    )(mine, quad, linear, offset)
    got = everyone(sent)
    for step in range(SINK - 1):
        resp, sent = call(
            functools.partial(balance_kernel, target), (resp_shape, sent_shape),
            2, 4 * area, 8 * area,
        )(got, resp)
        got = everyone(sent)
    sums = call(
        functools.partial(moment_kernel, target),
        jax.ShapeDtypeStruct((comp, 2 * width + LANES), F32), 5, 10 * big * comp,
        6 * big + 8 * area, scratch=[pltpu.VMEM((rows_dev, 2 * comp), BF16)],
    )(got, resp, mine, high, low)
    sent = sums.astype(jnp.float16).reshape(4, quarter, sums.shape[1])
    got = everyone(sent, axis_index_groups=blocks)
    sent = (SAFE * jnp.sum(got.astype(F32), axis=0)).astype(jnp.float16)
    got = everyone(sent.reshape(deep, quarter // deep, sent.shape[1]), axis_index_groups=lines)
    got = jnp.sum(got.astype(F32), axis=0)
    first, second = got[:, :width], got[:, width : 2 * width]
    units = (8.0, 2.0**-6, 2.0**-15, 2.0**-15)
    total = sum(u * got[:, 2 * width + 32 * i :][:, :1] for i, u in enumerate(units))
    new_mean = first / total
    new_var = second / total - new_mean * new_mean + 0.01
    done = jnp.concatenate([new_mean, new_var], axis=1).astype(jnp.float16)
    got = everyone(jnp.broadcast_to(done[None], (deep,) + done.shape), axis_index_groups=lines)
    here = got.reshape(1, quarter, 2 * width)
    got = everyone(jnp.broadcast_to(here, (4,) + here.shape[1:]), axis_index_groups=blocks)
    out = lax.optimization_barrier(got.reshape(comp, 2 * width))
    return (out[:, :width].astype(F32), out[:, width:].astype(F32))


def solution(mesh):
    return jax.shard_map(
        on_device,
        mesh=mesh,
        in_specs=(
            P(("wide", "narrow"), None),
            P(("wide", "narrow")),
            P("narrow", None),
            P("narrow", None),
        ),
        out_specs=(P("narrow", None), P("narrow", None)),
        check_vma=False,
    )
```
